32 devices in a mesh: dp: 4 (over y, x), fsdp: 8 (over z, core).
Axes of the slice: x: 2, y: 2, z: 4, core: 2. Of those that a mesh axis runs over, the one named last changes fastest.
Arguments:
- latents: float32 [128, 128, 384], P(('dp', 'fsdp')), may hold values from -6 to 6
- conditioning: float32 [128, 384], P(('dp', 'fsdp')), may hold values from -6 to 6
- counts: int32 [32], P(('dp', 'fsdp')), may hold values from 1 to 4, as said below
- cotangent: float32 [128, 128, 384], P(('dp', 'fsdp')), may hold values from -6 to 6
- ada_weights: bfloat16 [884736], P(('dp', 'fsdp')), may hold values from -0.3125 to 0.3125
- attn_weights: bfloat16 [589824], P(('dp', 'fsdp'))
- mlp_weights: bfloat16 [1179648], P(('dp', 'fsdp'))
- flat_biases: bfloat16 [5376], P(('dp', 'fsdp')), may hold values from -3 to 3
Outputs:
- output: float32 [128, 128, 384], P(('dp', 'fsdp'))
- grad_latents: float32 [128, 128, 384], P(('dp', 'fsdp'))
- grad_conditioning: float32 [128, 384], P(('dp', 'fsdp'))
- grad_ada_weights: float32 [884736], P(('dp', 'fsdp'))
- grad_attn_weights: float32 [589824], P(('dp', 'fsdp'))
- grad_mlp_weights: float32 [1179648], P(('dp', 'fsdp'))
- grad_biases: float32 [5376], P(('dp', 'fsdp'))
The draws below stay inside these ranges and needn't reach their ends.
Inputs may be any that keep to these rules, and one draw needn't show every extreme that they name: `counts`: slots of a device at or beyond its count hold padding; in every draw some device holds 4 live latents and some holds 1.
All inputs are finite; a program needn't handle non-finite values.
Results may differ from the reference program's by a relative error of at most 0.0095.
The reference program's roundings to bfloat16 on the way count: a program that leaves them out, or rounds other values in their place, can miss the bound.
Values may be sent and summed in bfloat16 or wider, within the bound.
A program may use at most 128 MiB of HBM per device.

```python
import jax
import jax.numpy as jnp
from jax import lax

D = 384
FF = 1536
HEADS = 6
SEQ = 128
LAT_CAP = 4
SHARDS = 32
SLOTS = 128
ADA_TOTAL = 884736
ATTN_TOTAL = 589824
MLP_TOTAL = 1179648
B_TOTAL = 5376


def draw_counts(key, part):
    first, second, third = jax.random.split(jax.random.fold_in(key, 11), 3)
    values = jax.random.randint(first, (SHARDS,), 1, LAT_CAP + 1, dtype=jnp.int32)
    busiest = jax.random.randint(second, (), 0, SHARDS, dtype=jnp.int32)
    lightest = (busiest + 1 + jax.random.randint(third, (), 0, SHARDS - 1, dtype=jnp.int32)) % SHARDS
    position = jnp.arange(SHARDS, dtype=jnp.int32)
    values = jnp.where(position == busiest, LAT_CAP, values)
    values = jnp.where(position == lightest, 1, values)
    return values.astype(jnp.int32)


def unit_values(key, total_count):
    values = jax.random.truncated_normal(key, -4.0, 4.0, (total_count,), jnp.float32)
    return values


def draw_attn_weights(key, part):
    position = jnp.arange(ATTN_TOTAL, dtype=jnp.int32)
    base = D ** (-0.5)
    spread = jnp.where(position < 3 * D * D, base, 6.0 * base)
    values = unit_values(jax.random.fold_in(key, 5), ATTN_TOTAL)
    return (values * spread).astype(jnp.bfloat16)


def draw_mlp_weights(key, part):
    position = jnp.arange(MLP_TOTAL, dtype=jnp.int32)
    spread = jnp.where(position < D * FF, D ** (-0.5), FF ** (-0.5))
    values = unit_values(jax.random.fold_in(key, 7), MLP_TOTAL)
    return (values * spread).astype(jnp.bfloat16)


def shard_levels(rng, extent, cuts, smallest, largest):
    level, own = 1.0, jax.random.fold_in(rng, 6)
    for dim, blocks in cuts:
        steps = jnp.exp(jax.random.uniform(jax.random.fold_in(own, dim), (blocks,), jnp.float32, smallest / len(cuts), largest / len(cuts)))
        level = level * jnp.repeat(steps, extent[dim] // blocks).reshape([-1 if axis == dim else 1 for axis in range(len(extent))])
    return level


def bell_draw(rng, extent, scale, reach, cuts=(), kind=jnp.bfloat16):
    level = shard_levels(rng, extent, cuts, -0.22, 0.18) if cuts else 1.0
    values = jax.random.normal(rng, extent, jnp.float32) * scale * level
    return jnp.minimum(jnp.maximum(values, -reach), reach).astype(kind)


def setup_inputs(seed: int = 0) -> dict:
    seeds = jax.random.split(jax.random.key(seed), 9)
    return {
        "latents": bell_draw(seeds[0], (SLOTS, SEQ, D), 1.0, 6.0, ((0, 32),), jnp.float32),
        "conditioning": bell_draw(seeds[1], (SLOTS, D), 1.0, 6.0, ((0, 32),), jnp.float32),
        "counts": draw_counts(jax.random.fold_in(seeds[8], 71), 0),
        "cotangent": bell_draw(seeds[3], (SLOTS, SEQ, D), 1.0, 6.0, ((0, 32),), jnp.float32),
        "ada_weights": bell_draw(seeds[4], (ADA_TOTAL,), D ** -0.5, 0.3125, ((0, 32),)),
        "attn_weights": draw_attn_weights(jax.random.fold_in(seeds[8], 71), 0),
        "mlp_weights": draw_mlp_weights(jax.random.fold_in(seeds[8], 71), 0),
        "flat_biases": bell_draw(seeds[7], (B_TOTAL,), 0.5, 3.0, ((0, 32),)),
    }


EPSILON = 1e-06
GELU_COEF = 0.044715
ROOT_TWO_OVER_PI = 0.7978845608028654

def layer_norm(values):
    centre = values - lax.optimization_barrier(jnp.mean(values, axis=-1, keepdims=True))
    inverse = lax.rsqrt(lax.optimization_barrier(jnp.mean(centre * centre, axis=-1, keepdims=True)) + EPSILON)
    return (centre * inverse, inverse)

def norm_backward(grad_norm, normed, inverse):
    first = lax.optimization_barrier(jnp.mean(grad_norm, axis=-1, keepdims=True))
    second = lax.optimization_barrier(jnp.mean(grad_norm * normed, axis=-1, keepdims=True))
    return (grad_norm - first - normed * second) * inverse

def gelu_value(pre_act):
    inner = ROOT_TWO_OVER_PI * (pre_act + GELU_COEF * pre_act * pre_act * pre_act)
    return 0.5 * pre_act * (1.0 + jnp.tanh(inner))

def gelu_slope(pre_act):
    tanh_part = jnp.tanh(ROOT_TWO_OVER_PI * (pre_act + GELU_COEF * pre_act * pre_act * pre_act))
    return 0.5 * (1.0 + tanh_part) + 0.5 * pre_act * (1.0 - tanh_part * tanh_part) * ROOT_TWO_OVER_PI * (1.0 + 3.0 * GELU_COEF * pre_act * pre_act)

def silu_slope(values):
    sigma = jax.nn.sigmoid(values)
    return sigma * (1.0 + values * (1.0 - sigma))

def product(form, left, right):
    return jnp.einsum(form, left.astype(jnp.float32), right.astype(jnp.float32))

def mat_dot(left, right):
    return jnp.dot(left, right, preferred_element_type=jnp.float32)

def unpack(ada_flat, attn_flat, mlp_flat, bias_flat, model_width, hidden_units):
    qkv_size = 3 * model_width * model_width
    fc1_size = model_width * hidden_units
    pieces = [ada_flat.reshape(model_width, 6 * model_width), attn_flat[:qkv_size].reshape(model_width, 3 * model_width), attn_flat[qkv_size:].reshape(model_width, model_width), mlp_flat[:fc1_size].reshape(model_width, hidden_units), mlp_flat[fc1_size:].reshape(hidden_units, model_width)]
    offset = 0
    for extent_now in [6 * model_width, model_width, model_width, model_width, hidden_units, model_width]:
        pieces.append(bias_flat[offset:offset + extent_now])
        offset = offset + extent_now
    return tuple(pieces)

def forward_group(latent_rows, cond_rows, live_rows, weights, head_count):
    w_ada, w_qkv, w_proj, w_fc1, w_fc2, b_ada, b_query, b_value, b_proj, b_fc1, b_fc2 = weights
    groups, length, model_width = latent_rows.shape
    head_dim = model_width // head_count
    row_count = groups * length
    score_scale = head_dim ** (-0.5)
    cond_act = jax.nn.silu(cond_rows).astype(jnp.bfloat16)
    modulation = mat_dot(cond_act, w_ada) + b_ada.astype(jnp.float32)
    parts = [modulation[:, None, k * model_width:(k + 1) * model_width] for k in range(6)]
    shift_attn, scale_attn, gate_attn, shift_mlp, scale_mlp, gate_mlp = parts
    norm_one, inverse_one = layer_norm(latent_rows)
    modulated_one = (norm_one * (1.0 + scale_attn) + shift_attn).astype(jnp.bfloat16)
    projected = mat_dot(modulated_one.reshape(row_count, model_width), w_qkv)
    query_rows = (projected[:, :model_width] + b_query.astype(jnp.float32)).astype(jnp.bfloat16).reshape(groups, length, model_width)
    key_rows = projected[:, model_width:2 * model_width].astype(jnp.bfloat16).reshape(groups, length, model_width)
    value_rows = (projected[:, 2 * model_width:] + b_value.astype(jnp.float32)).astype(jnp.bfloat16).reshape(groups, length, model_width)
    split_shape = (groups, length, head_count, head_dim)
    scores = product('gqhe,gkhe->ghqk', query_rows.reshape(split_shape), key_rows.reshape(split_shape)) * score_scale
    log_total = jnp.log(lax.optimization_barrier(jnp.sum(jnp.exp(scores), axis=-1, keepdims=True)))
    probs = jnp.exp(scores - log_total).astype(jnp.bfloat16)
    mixed = product('ghqk,gkhe->gqhe', probs, value_rows.reshape(split_shape)).astype(jnp.bfloat16).reshape(row_count, model_width)
    branch = (mat_dot(mixed, w_proj) + b_proj.astype(jnp.float32)).reshape(groups, length, model_width)
    after_attn = latent_rows + gate_attn * branch
    norm_two, inverse_two = layer_norm(after_attn)
    modulated_two = (norm_two * (1.0 + scale_mlp) + shift_mlp).astype(jnp.bfloat16)
    pre_act = mat_dot(modulated_two.reshape(row_count, model_width), w_fc1) + b_fc1.astype(jnp.float32)
    activated = gelu_value(pre_act).astype(jnp.bfloat16)
    mlp_rows = (mat_dot(activated, w_fc2) + b_fc2.astype(jnp.float32)).reshape(groups, length, model_width)
    output = jnp.where(live_rows[:, None, None], after_attn + gate_mlp * mlp_rows, 0.0)
    hidden_units = pre_act.shape[1]
    saved = (cond_act, modulation, norm_one, inverse_one, modulated_one, query_rows, key_rows, value_rows, log_total[..., 0], mixed.reshape(groups, length, model_width), branch, norm_two, inverse_two, modulated_two, pre_act.reshape(groups, length, hidden_units), activated.reshape(groups, length, hidden_units), mlp_rows)
    return (output, saved)

def mlp_backward(saved, cotangent_rows, live_rows, weights):
    w_fc1 = weights[3]
    w_fc2 = weights[4]
    cond_act, modulation, norm_one, inverse_one, modulated_one, query_rows, key_rows, value_rows, log_total, mixed, branch, norm_two, inverse_two, modulated_two, pre_act, activated, mlp_rows = saved
    groups, length, model_width = cotangent_rows.shape
    hidden_units = pre_act.shape[2]
    row_count = groups * length
    scale_mlp = modulation[:, None, 4 * model_width:5 * model_width]
    gate_mlp = modulation[:, None, 5 * model_width:6 * model_width]
    grad_out = jnp.where(live_rows[:, None, None], cotangent_rows, 0.0)
    grad_gate_mlp = lax.optimization_barrier(jnp.sum(grad_out * mlp_rows, axis=1))
    grad_mlp_full = grad_out * gate_mlp
    bias_fc2 = lax.optimization_barrier(jnp.sum(grad_mlp_full, axis=(0, 1)))
    grad_mlp = grad_mlp_full.astype(jnp.bfloat16).reshape(row_count, model_width)
    weight_fc2 = mat_dot(activated.reshape(row_count, hidden_units).T, grad_mlp)
    grad_pre_full = mat_dot(grad_mlp, w_fc2.T) * gelu_slope(pre_act.reshape(row_count, hidden_units))
    bias_fc1 = lax.optimization_barrier(jnp.sum(grad_pre_full, axis=0))
    grad_pre = grad_pre_full.astype(jnp.bfloat16)
    weight_fc1 = mat_dot(modulated_two.reshape(row_count, model_width).T, grad_pre)
    grad_two = mat_dot(grad_pre, w_fc1.T).reshape(groups, length, model_width)
    grad_scale_mlp = lax.optimization_barrier(jnp.sum(grad_two * norm_two, axis=1))
    grad_shift_mlp = lax.optimization_barrier(jnp.sum(grad_two, axis=1))
    grad_after = grad_out + norm_backward(grad_two * (1.0 + scale_mlp), norm_two, inverse_two)
    mod_tail = jnp.concatenate([grad_shift_mlp, grad_scale_mlp, grad_gate_mlp], axis=1)
    return (grad_after, mod_tail, (weight_fc1, weight_fc2, bias_fc1, bias_fc2))

def attention_backward(saved, cond_rows, grad_after, mod_tail, weights, head_count):
    w_ada = weights[0]
    w_qkv = weights[1]
    w_proj = weights[2]
    cond_act, modulation, norm_one, inverse_one, modulated_one, query_rows, key_rows, value_rows, log_total, mixed, branch, norm_two, inverse_two, modulated_two, pre_act, activated, mlp_rows = saved
    groups, length, model_width = grad_after.shape
    head_dim = model_width // head_count
    row_count = groups * length
    score_scale = head_dim ** (-0.5)
    scale_attn = modulation[:, None, model_width:2 * model_width]
    gate_attn = modulation[:, None, 2 * model_width:3 * model_width]
    grad_gate_attn = lax.optimization_barrier(jnp.sum(grad_after * branch, axis=1))
    grad_branch_full = grad_after * gate_attn
    bias_proj = lax.optimization_barrier(jnp.sum(grad_branch_full, axis=(0, 1)))
    grad_branch = grad_branch_full.astype(jnp.bfloat16).reshape(row_count, model_width)
    weight_proj = mat_dot(mixed.reshape(row_count, model_width).T, grad_branch)
    grad_mixed = mat_dot(grad_branch, w_proj.T).astype(jnp.bfloat16)
    split_shape = (groups, length, head_count, head_dim)
    query_split = query_rows.reshape(split_shape)
    key_split = key_rows.reshape(split_shape)
    value_split = value_rows.reshape(split_shape)
    mixed_split = grad_mixed.reshape(split_shape)
    scores = product('gqhe,gkhe->ghqk', query_split, key_split) * score_scale
    probs_full = jnp.exp(scores - log_total[..., None])
    grad_probs = product('gqhe,gkhe->ghqk', mixed_split, value_split)
    grad_value = product('ghqk,gqhe->gkhe', probs_full.astype(jnp.bfloat16), mixed_split).astype(jnp.bfloat16)
    delta_rows = lax.optimization_barrier(jnp.sum(probs_full * grad_probs, axis=-1, keepdims=True))
    grad_scores = (probs_full * (grad_probs - delta_rows) * score_scale).astype(jnp.bfloat16)
    grad_query = product('ghqk,gkhe->gqhe', grad_scores, key_split).astype(jnp.bfloat16)
    grad_key = product('ghqk,gqhe->gkhe', grad_scores, query_split).astype(jnp.bfloat16)
    grad_query = grad_query.reshape(row_count, model_width)
    grad_key = grad_key.reshape(row_count, model_width)
    grad_value = grad_value.reshape(row_count, model_width)
    grad_proj_in = jnp.concatenate([grad_query, grad_key, grad_value], axis=1)
    weight_qkv = mat_dot(modulated_one.reshape(row_count, model_width).T, grad_proj_in)
    bias_query = lax.optimization_barrier(jnp.sum(grad_query.astype(jnp.float32), axis=0))
    bias_value = lax.optimization_barrier(jnp.sum(grad_value.astype(jnp.float32), axis=0))
    grad_one = mat_dot(grad_proj_in, w_qkv.T).reshape(groups, length, model_width)
    grad_scale_attn = lax.optimization_barrier(jnp.sum(grad_one * norm_one, axis=1))
    grad_shift_attn = lax.optimization_barrier(jnp.sum(grad_one, axis=1))
    grad_input = grad_after + norm_backward(grad_one * (1.0 + scale_attn), norm_one, inverse_one)
    grad_mod_full = jnp.concatenate([grad_shift_attn, grad_scale_attn, grad_gate_attn, mod_tail], axis=1)
    bias_ada = lax.optimization_barrier(jnp.sum(grad_mod_full, axis=0))
    grad_mod = grad_mod_full.astype(jnp.bfloat16)
    weight_ada = mat_dot(cond_act.T, grad_mod)
    grad_cond = mat_dot(grad_mod, w_ada.T) * silu_slope(cond_rows)
    return (grad_input, grad_cond, (weight_ada, weight_qkv, weight_proj, bias_ada, bias_query, bias_value, bias_proj))

def reference(latents, conditioning, counts, cotangent, ada_weights, attn_weights, mlp_weights, flat_biases):
    weights = unpack(ada_weights, attn_weights, mlp_weights, flat_biases, D, FF)
    slot_count = latents.shape[0]
    slot_ids = jnp.arange(slot_count, dtype=jnp.int32)
    live = slot_ids % LAT_CAP < counts[slot_ids // LAT_CAP]
    group_size = 16
    turns = slot_count // group_size

    def grouped(array):
        return array.reshape((turns, group_size) + array.shape[1:])
    zero_attn = tuple((jnp.zeros(weights[k].shape, jnp.float32) for k in (0, 1, 2, 5, 6, 7, 8)))
    zero_mlp = tuple((jnp.zeros(weights[k].shape, jnp.float32) for k in (3, 4, 9, 10)))

    def step(totals, inputs):
        attn_totals, mlp_totals = totals
        latent_rows, cond_rows, cotangent_rows, live_rows = inputs
        output, saved = forward_group(latent_rows, cond_rows, live_rows, weights, HEADS)
        grad_after, mod_tail, mlp_grads = mlp_backward(saved, cotangent_rows, live_rows, weights)
        grad_input, grad_cond, attn_grads = attention_backward(saved, cond_rows, grad_after, mod_tail, weights, HEADS)
        attn_totals = tuple((total + grad for total, grad in zip(attn_totals, attn_grads)))
        mlp_totals = tuple((total + grad for total, grad in zip(mlp_totals, mlp_grads)))
        return ((attn_totals, mlp_totals), (output, grad_input, grad_cond))
    totals, stacked = lax.scan(step, (zero_attn, zero_mlp), (grouped(latents), grouped(conditioning), grouped(cotangent), grouped(live)))
    attn_totals, mlp_totals = totals
    output = stacked[0].reshape(latents.shape)
    grad_latents = stacked[1].reshape(latents.shape)
    grad_conditioning = stacked[2].reshape(conditioning.shape)
    grad_ada = attn_totals[0].reshape(-1)
    grad_attn = jnp.concatenate([attn_totals[1].reshape(-1), attn_totals[2].reshape(-1)])
    grad_mlp = jnp.concatenate([mlp_totals[0].reshape(-1), mlp_totals[1].reshape(-1)])
    grad_biases = jnp.concatenate([attn_totals[3], attn_totals[4], attn_totals[5], attn_totals[6], mlp_totals[2], mlp_totals[3]])
    return (output, grad_latents, grad_conditioning, grad_ada, grad_attn, grad_mlp, grad_biases)
```

```python
from functools import partial
import math

import jax
import jax.numpy as jnp
from jax import lax
from jax.experimental import pallas as pl
from jax.experimental.pallas import tpu as pltpu
from jax.sharding import PartitionSpec as P

FF = 1536
HEADS = 6


EPSILON = 1e-06
GELU_COEF = 0.044715
ROOT_TWO_OVER_PI = 0.7978845608028654


def layer_norm(values):
    centre = values - jnp.mean(values, axis=-1, keepdims=True)
    inverse = lax.rsqrt(jnp.mean(centre * centre, axis=-1, keepdims=True) + EPSILON)
    return (centre * inverse, inverse)


def norm_backward(grad_norm, normed, inverse):
    first = jnp.mean(grad_norm, axis=-1, keepdims=True)
    second = jnp.mean(grad_norm * normed, axis=-1, keepdims=True)
    return (grad_norm - first - normed * second) * inverse


def gelu_value(pre_act):
    inner = ROOT_TWO_OVER_PI * (pre_act + GELU_COEF * pre_act * pre_act * pre_act)
    return 0.5 * pre_act * (1.0 + jnp.tanh(inner))


def gelu_slope(pre_act):
    tanh_part = jnp.tanh(ROOT_TWO_OVER_PI * (pre_act + GELU_COEF * pre_act * pre_act * pre_act))
    return 0.5 * (1.0 + tanh_part) + 0.5 * pre_act * (
        1.0 - tanh_part * tanh_part
    ) * ROOT_TWO_OVER_PI * (1.0 + 3.0 * GELU_COEF * pre_act * pre_act)


def silu_slope(values):
    sigma = jax.nn.sigmoid(values)
    return sigma * (1.0 + values * (1.0 - sigma))


def product(form, left, right):
    return jnp.einsum(form, left, right, preferred_element_type=jnp.float32)


def mat_dot(left, right):
    return jnp.dot(left, right, preferred_element_type=jnp.float32)


def unpack(ada_flat, attn_flat, mlp_flat, bias_flat, model_width, hidden_units):
    qkv_size = 3 * model_width * model_width
    fc1_size = model_width * hidden_units
    pieces = [
        ada_flat.reshape(model_width, 6 * model_width),
        attn_flat[:qkv_size].reshape(model_width, 3 * model_width),
        attn_flat[qkv_size:].reshape(model_width, model_width),
        mlp_flat[:fc1_size].reshape(model_width, hidden_units),
        mlp_flat[fc1_size:].reshape(hidden_units, model_width),
    ]
    offset = 0
    for extent_now in [
        6 * model_width,
        model_width,
        model_width,
        model_width,
        hidden_units,
        model_width,
    ]:
        pieces.append(bias_flat[offset : offset + extent_now])
        offset = offset + extent_now
    return tuple(pieces)


def forward_group(latent_rows, cond_rows, live_rows, weights, head_count):
    w_ada, w_qkv, w_proj, w_fc1, w_fc2, b_ada, b_query, b_value, b_proj, b_fc1, b_fc2 = weights
    groups, length, model_width = latent_rows.shape
    head_dim = model_width // head_count
    row_count = groups * length
    score_scale = head_dim ** (-0.5)
    cond_act = jax.nn.silu(cond_rows).astype(jnp.bfloat16)
    modulation = mat_dot(cond_act, w_ada) + b_ada.astype(jnp.float32)
    parts = [modulation[:, None, k * model_width : (k + 1) * model_width] for k in range(6)]
    shift_attn, scale_attn, gate_attn, shift_mlp, scale_mlp, gate_mlp = parts
    norm_one, inverse_one = layer_norm(latent_rows)
    modulated_one = (norm_one * (1.0 + scale_attn) + shift_attn).astype(jnp.bfloat16)
    projected = mat_dot(modulated_one.reshape(row_count, model_width), w_qkv)
    query_rows = (
        (projected[:, :model_width] + b_query.astype(jnp.float32))
        .astype(jnp.bfloat16)
        .reshape(groups, length, model_width)
    )
    key_rows = (
        projected[:, model_width : 2 * model_width]
        .astype(jnp.bfloat16)
        .reshape(groups, length, model_width)
    )
    value_rows = (
        (projected[:, 2 * model_width :] + b_value.astype(jnp.float32))
        .astype(jnp.bfloat16)
        .reshape(groups, length, model_width)
    )
    split_shape = (groups, length, head_count, head_dim)
    scores = (
        product("gqhe,gkhe->ghqk", query_rows.reshape(split_shape), key_rows.reshape(split_shape))
        * score_scale
    )
    log_total = jnp.log(jnp.sum(jnp.exp(scores), axis=-1, keepdims=True))
    probs = jnp.exp(scores - log_total).astype(jnp.bfloat16)
    mixed = (
        product("ghqk,gkhe->gqhe", probs, value_rows.reshape(split_shape))
        .astype(jnp.bfloat16)
        .reshape(row_count, model_width)
    )
    branch = (mat_dot(mixed, w_proj) + b_proj.astype(jnp.float32)).reshape(
        groups, length, model_width
    )
    after_attn = latent_rows + gate_attn * branch
    norm_two, inverse_two = layer_norm(after_attn)
    modulated_two = (norm_two * (1.0 + scale_mlp) + shift_mlp).astype(jnp.bfloat16)
    pre_act = mat_dot(modulated_two.reshape(row_count, model_width), w_fc1) + b_fc1.astype(
        jnp.float32
    )
    activated = gelu_value(pre_act).astype(jnp.bfloat16)
    mlp_rows = (mat_dot(activated, w_fc2) + b_fc2.astype(jnp.float32)).reshape(
        groups, length, model_width
    )
    output = jnp.where(live_rows[:, None, None], after_attn + gate_mlp * mlp_rows, 0.0)
    hidden_units = pre_act.shape[1]
    saved = (
        cond_act,
        modulation,
        norm_one,
        inverse_one,
        modulated_one,
        query_rows,
        key_rows,
        value_rows,
        log_total[..., 0],
        mixed.reshape(groups, length, model_width),
        branch,
        norm_two,
        inverse_two,
        modulated_two,
        pre_act.reshape(groups, length, hidden_units),
        activated.reshape(groups, length, hidden_units),
        mlp_rows,
    )
    return (output, saved)


def mlp_backward(saved, cotangent_rows, live_rows, weights):
    w_fc1 = weights[3]
    w_fc2 = weights[4]
    (
        cond_act,
        modulation,
        norm_one,
        inverse_one,
        modulated_one,
        query_rows,
        key_rows,
        value_rows,
        log_total,
        mixed,
        branch,
        norm_two,
        inverse_two,
        modulated_two,
        pre_act,
        activated,
        mlp_rows,
    ) = saved
    groups, length, model_width = cotangent_rows.shape
    hidden_units = pre_act.shape[2]
    row_count = groups * length
    scale_mlp = modulation[:, None, 4 * model_width : 5 * model_width]
    gate_mlp = modulation[:, None, 5 * model_width : 6 * model_width]
    grad_out = jnp.where(live_rows[:, None, None], cotangent_rows, 0.0)
    grad_gate_mlp = jnp.sum(grad_out * mlp_rows, axis=1)
    grad_mlp_full = grad_out * gate_mlp
    bias_fc2 = jnp.sum(grad_mlp_full, axis=(0, 1))
    grad_mlp = grad_mlp_full.astype(jnp.bfloat16).reshape(row_count, model_width)
    weight_fc2 = mat_dot(activated.reshape(row_count, hidden_units).T, grad_mlp)
    grad_pre_full = mat_dot(grad_mlp, w_fc2.T) * gelu_slope(
        pre_act.reshape(row_count, hidden_units)
    )
    bias_fc1 = jnp.sum(grad_pre_full, axis=0)
    grad_pre = grad_pre_full.astype(jnp.bfloat16)
    weight_fc1 = mat_dot(modulated_two.reshape(row_count, model_width).T, grad_pre)
    grad_two = mat_dot(grad_pre, w_fc1.T).reshape(groups, length, model_width)
    grad_scale_mlp = jnp.sum(grad_two * norm_two, axis=1)
    grad_shift_mlp = jnp.sum(grad_two, axis=1)
    grad_after = grad_out + norm_backward(grad_two * (1.0 + scale_mlp), norm_two, inverse_two)
    mod_tail = jnp.concatenate([grad_shift_mlp, grad_scale_mlp, grad_gate_mlp], axis=1)
    return (grad_after, mod_tail, (weight_fc1, weight_fc2, bias_fc1, bias_fc2))


def attention_backward(saved, cond_rows, grad_after, mod_tail, weights, head_count):
    w_ada = weights[0]
    w_qkv = weights[1]
    w_proj = weights[2]
    (
        cond_act,
        modulation,
        norm_one,
        inverse_one,
        modulated_one,
        query_rows,
        key_rows,
        value_rows,
        log_total,
        mixed,
        branch,
        norm_two,
        inverse_two,
        modulated_two,
        pre_act,
        activated,
        mlp_rows,
    ) = saved
    groups, length, model_width = grad_after.shape
    head_dim = model_width // head_count
    row_count = groups * length
    score_scale = head_dim ** (-0.5)
    scale_attn = modulation[:, None, model_width : 2 * model_width]
    gate_attn = modulation[:, None, 2 * model_width : 3 * model_width]
    grad_gate_attn = jnp.sum(grad_after * branch, axis=1)
    grad_branch_full = grad_after * gate_attn
    bias_proj = jnp.sum(grad_branch_full, axis=(0, 1))
    grad_branch = grad_branch_full.astype(jnp.bfloat16).reshape(row_count, model_width)
    weight_proj = mat_dot(mixed.reshape(row_count, model_width).T, grad_branch)
    grad_mixed = mat_dot(grad_branch, w_proj.T).astype(jnp.bfloat16)
    split_shape = (groups, length, head_count, head_dim)
    query_split = query_rows.reshape(split_shape)
    key_split = key_rows.reshape(split_shape)
    value_split = value_rows.reshape(split_shape)
    mixed_split = grad_mixed.reshape(split_shape)
    scores = product("gqhe,gkhe->ghqk", query_split, key_split) * score_scale
    probs_full = jnp.exp(scores - log_total[..., None])
    grad_probs = product("gqhe,gkhe->ghqk", mixed_split, value_split)
    grad_value = product("ghqk,gqhe->gkhe", probs_full.astype(jnp.bfloat16), mixed_split).astype(
        jnp.bfloat16
    )
    delta_rows = jnp.sum(probs_full * grad_probs, axis=-1, keepdims=True)
    grad_scores = (probs_full * (grad_probs - delta_rows) * score_scale).astype(jnp.bfloat16)
    grad_query = product("ghqk,gkhe->gqhe", grad_scores, key_split).astype(jnp.bfloat16)
    grad_key = product("ghqk,gqhe->gkhe", grad_scores, query_split).astype(jnp.bfloat16)
    grad_query = grad_query.reshape(row_count, model_width)
    grad_key = grad_key.reshape(row_count, model_width)
    grad_value = grad_value.reshape(row_count, model_width)
    grad_proj_in = jnp.concatenate([grad_query, grad_key, grad_value], axis=1)
    weight_qkv = mat_dot(modulated_one.reshape(row_count, model_width).T, grad_proj_in)
    bias_query = jnp.sum(grad_query.astype(jnp.float32), axis=0)
    bias_value = jnp.sum(grad_value.astype(jnp.float32), axis=0)
    grad_one = mat_dot(grad_proj_in, w_qkv.T).reshape(groups, length, model_width)
    grad_scale_attn = jnp.sum(grad_one * norm_one, axis=1)
    grad_shift_attn = jnp.sum(grad_one, axis=1)
    grad_input = grad_after + norm_backward(grad_one * (1.0 + scale_attn), norm_one, inverse_one)
    grad_mod_full = jnp.concatenate(
        [grad_shift_attn, grad_scale_attn, grad_gate_attn, mod_tail], axis=1
    )
    bias_ada = jnp.sum(grad_mod_full, axis=0)
    grad_mod = grad_mod_full.astype(jnp.bfloat16)
    weight_ada = mat_dot(cond_act.T, grad_mod)
    grad_cond = mat_dot(grad_mod, w_ada.T) * silu_slope(cond_rows)
    return (
        grad_input,
        grad_cond,
        (weight_ada, weight_qkv, weight_proj, bias_ada, bias_query, bias_value, bias_proj),
    )


LANES = 128
SUBLANES = 16
AXES = ("dp", "fsdp")
MESH = pl.DeviceIdType.MESH


class Grid:
    def __init__(self, mesh):
        dp, fsdp = mesh.shape["dp"], mesh.shape["fsdp"]
        side = math.isqrt(dp)
        self.high = side if side * side == dp else 1
        self.low = dp // self.high
        self.pair = 2 if fsdp % 2 == 0 else 1
        self.depth = fsdp // self.pair
        self.count = dp * fsdp
        self.sizes = (self.high, self.low, self.depth, self.pair)

    def here(self):
        a, f = lax.axis_index("dp"), lax.axis_index("fsdp")
        return [a // self.low, a % self.low, f // self.pair, f % self.pair]

    def peer(self, here, axis, step):
        spot = list(here)
        spot[axis] = lax.rem(here[axis] + step, self.sizes[axis])
        return spot

    def ident(self, spot):
        return (spot[0] * self.low + spot[1], spot[2] * self.pair + spot[3])

    def barrier(self, here):
        sem = pltpu.get_barrier_semaphore()
        total = 0
        for axis in range(4):
            for step in range(1, self.sizes[axis]):
                pl.semaphore_signal(
                    sem, inc=1, device_id=self.ident(self.peer(here, axis, step)), device_id_type=MESH
                )
                total += 1
        pl.semaphore_wait(sem, total)


def split_rows(rows, parts):
    units = rows // SUBLANES
    parts = min(parts, units)
    cuts = [units * k // parts for k in range(parts + 1)]
    return [(cuts[k] * SUBLANES, (cuts[k + 1] - cuts[k]) * SUBLANES) for k in range(parts)]


def gather_kernel(grid, chunks, in_ref, out_ref, send_sem, recv_sem, own_sem):
    here = grid.here()
    hi, lo, z, c = here
    spare = iter(range(send_sem.shape[0]))
    grid.barrier(here)

    def push(src, dst, spot):
        k = next(spare)
        copy = pltpu.make_async_remote_copy(
            src_ref=src, dst_ref=dst, send_sem=send_sem.at[k], recv_sem=recv_sem.at[k],
            device_id=grid.ident(spot), device_id_type=MESH,
        )
        copy.start()
        return copy

    def steps(axis):
        return [grid.peer(here, axis, s) for s in range(1, grid.sizes[axis])]

    everything = []

    def pushes(src, dst, spots):
        copies = [push(src, dst, spot) for spot in spots]
        everything.extend(copies)
        return copies

    def arrive(copies):
        for copy in copies:
            copy.wait_recv()

    own = pltpu.make_async_copy(in_ref, out_ref.at[hi, lo, z, c], own_sem)
    own.start()
    along_z, first, second, swap = [], [], [], []
    for start, size in chunks:
        rows = pl.ds(start, size)
        along_z.append(pushes(in_ref.at[rows], out_ref.at[hi, lo, z, c, rows], steps(2)))
    own.wait()
    for k, (start, size) in enumerate(chunks):
        rows = pl.ds(start, size)
        arrive(along_z[k])
        part = out_ref.at[hi, lo, :, c, rows]
        first.append(pushes(part, part, steps(1 if k % 2 == 0 else 0)))
        swap += pushes(part, part, steps(3))
    for k, (start, size) in enumerate(chunks):
        rows = pl.ds(start, size)
        arrive(first[k])
        if k % 2 == 0:
            part = out_ref.at[hi, :, :, c, rows]
            second.append(pushes(part, part, steps(0)))
            others = [out_ref.at[hi, spot[1], :, c, rows] for spot in steps(1)]
        else:
            part = out_ref.at[:, lo, :, c, rows]
            second.append(pushes(part, part, steps(1)))
            others = [out_ref.at[spot[0], lo, :, c, rows] for spot in steps(0)]
        for other in others:
            swap += pushes(other, other, steps(3))
    for k, (start, size) in enumerate(chunks):
        rows = pl.ds(start, size)
        arrive(second[k])
        if k % 2 == 0:
            others = [out_ref.at[spot[0], :, :, c, rows] for spot in steps(0)]
        else:
            others = [out_ref.at[:, spot[1], :, c, rows] for spot in steps(1)]
        for other in others:
            swap += pushes(other, other, steps(3))
    arrive(swap)
    for copy in everything:
        copy.wait_send()


def gather_copies(grid, chunk_count):
    high, low, depth, pair = grid.sizes
    first = lambda k: low - 1 if k % 2 == 0 else high - 1
    second = lambda k: high - 1 if k % 2 == 0 else low - 1
    return sum(
        (depth - 1) + first(k) + second(k) + (pair - 1) * (1 + first(k) + second(k))
        for k in range(chunk_count)
    )


def gather_all(grid, slab):
    rows = slab.shape[0]
    chunks = split_rows(rows, 4)
    copies = gather_copies(grid, len(chunks))
    return pl.pallas_call(
        partial(gather_kernel, grid, chunks),
        out_shape=jax.ShapeDtypeStruct(grid.sizes + slab.shape, slab.dtype),
        in_specs=[pl.BlockSpec(memory_space=pltpu.VMEM)],
        out_specs=pl.BlockSpec(memory_space=pltpu.VMEM),
        scratch_shapes=[
            pltpu.SemaphoreType.DMA((copies,)),
            pltpu.SemaphoreType.DMA((copies,)),
            pltpu.SemaphoreType.DMA,
        ],
        compiler_params=pltpu.CompilerParams(
            collective_id=0, has_side_effects=True, vmem_limit_bytes=48 * 1024 * 1024
        ),
    )(slab)


def scatter_kernel(
    grid, chunks, g_ref, out_ref, pair_buf, acc, buf_one, buf_two, buf_z, send_sem, recv_sem
):
    here = grid.here()
    hi, lo, z, c = here
    spare = iter(range(send_sem.shape[0]))
    grid.barrier(here)
    everything = []

    def push(src, dst, spot):
        k = next(spare)
        copy = pltpu.make_async_remote_copy(
            src_ref=src, dst_ref=dst, send_sem=send_sem.at[k], recv_sem=recv_sem.at[k],
            device_id=grid.ident(spot), device_id_type=MESH,
        )
        copy.start()
        everything.append(copy)
        return copy

    def steps(axis):
        return [(s - 1, grid.peer(here, axis, s)) for s in range(1, grid.sizes[axis])]

    def arrive(copies):
        for copy in copies:
            copy.wait_recv()

    def add(into, terms, first, second):
        def body(t, _):
            i, j = t // second, t % second
            total = terms[0](i, j)[...].astype(jnp.float32)
            for term in terms[1:]:
                total = total + term(i, j)[...].astype(jnp.float32)
            target = into(i, j)
            target[...] = total.astype(target.dtype)
            return 0

        lax.fori_loop(0, first * second, body, 0)

    high, low, depth, pair = grid.sizes
    swaps, ones, twos, lines = [], [], [], []
    for start, size in chunks:
        rows = pl.ds(start, size)
        swaps.append(
            [push(g_ref.at[:, :, :, spot[3], rows], pair_buf.at[:, :, :, rows], spot) for _, spot in steps(3)]
        )
    for k, (start, size) in enumerate(chunks):
        rows = pl.ds(start, size)
        arrive(swaps[k])
        terms = [lambda i, j: g_ref.at[i // low, i % low, j, c, rows]]
        if pair > 1:
            terms.append(lambda i, j: pair_buf.at[i // low, i % low, j, rows])
        add(lambda i, j: acc.at[i // low, i % low, j, rows], terms, high * low, depth)
        if k % 2 == 0:
            ones.append(
                [push(acc.at[spot[0], :, :, rows], buf_one.at[s, 0:low, :, rows], spot) for s, spot in steps(0)]
            )
        else:
            ones.append(
                [push(acc.at[:, spot[1], :, rows], buf_one.at[s, 0:high, :, rows], spot) for s, spot in steps(1)]
            )
    for k, (start, size) in enumerate(chunks):
        rows = pl.ds(start, size)
        arrive(ones[k])
        even = k % 2 == 0
        mine = (lambda i, j: acc.at[hi, i, j, rows]) if even else (lambda i, j: acc.at[i, lo, j, rows])
        terms = [mine] + [
            (lambda i, j, s=s: buf_one.at[s, i, j, rows]) for s, _ in steps(0 if even else 1)
        ]
        add(mine, terms, low if even else high, depth)
        if even:
            twos.append(
                [push(acc.at[hi, spot[1], :, rows], buf_two.at[s, :, rows], spot) for s, spot in steps(1)]
            )
        else:
            twos.append(
                [push(acc.at[spot[0], lo, :, rows], buf_two.at[s, :, rows], spot) for s, spot in steps(0)]
            )
    for k, (start, size) in enumerate(chunks):
        rows = pl.ds(start, size)
        arrive(twos[k])
        mine = lambda i, j: acc.at[hi, lo, j, rows]
        terms = [mine] + [
            (lambda i, j, s=s: buf_two.at[s, j, rows]) for s, _ in steps(1 if k % 2 == 0 else 0)
        ]
        add(mine, terms, 1, depth)
        lines.append(
            [push(acc.at[hi, lo, spot[2], rows], buf_z.at[s, rows], spot) for s, spot in steps(2)]
        )
    for k, (start, size) in enumerate(chunks):
        rows = pl.ds(start, size)
        arrive(lines[k])
        total = acc[hi, lo, z, rows].astype(jnp.float32)
        for s in range(depth - 1):
            total = total + buf_z[s, rows].astype(jnp.float32)
        out_ref[rows, :] = total
    for copy in everything:
        copy.wait_send()


def scatter_sum(grid, packed):
    high, low, depth, pair = grid.sizes
    rows, lanes = packed.shape[-2:]
    chunks = split_rows(rows, 4)
    copies = len(chunks) * (high + low + depth + pair - 4)
    kind = packed.dtype
    return pl.pallas_call(
        partial(scatter_kernel, grid, chunks),
        out_shape=jax.ShapeDtypeStruct((rows, lanes), jnp.float32),
        in_specs=[pl.BlockSpec(memory_space=pltpu.VMEM)],
        out_specs=pl.BlockSpec(memory_space=pltpu.VMEM),
        scratch_shapes=[
            pltpu.VMEM((high, low, depth, rows, lanes), kind),
            pltpu.VMEM((high, low, depth, rows, lanes), kind),
            pltpu.VMEM((max(high, low) - 1, max(high, low), depth, rows, lanes), kind),
            pltpu.VMEM((max(high, low) - 1, depth, rows, lanes), kind),
            pltpu.VMEM((max(depth - 1, 1), rows, lanes), kind),
            pltpu.SemaphoreType.DMA((copies,)),
            pltpu.SemaphoreType.DMA((copies,)),
        ],
        compiler_params=pltpu.CompilerParams(
            collective_id=1, has_side_effects=True, vmem_limit_bytes=48 * 1024 * 1024
        ),
    )(packed)


def padded_rows(extent):
    return -(-extent // LANES)


def pack(pieces, lead):
    parts = []
    for piece in pieces:
        extent = piece.shape[-1]
        rows = padded_rows(extent)
        gap = rows * LANES - extent
        if gap:
            piece = jnp.pad(piece, [(0, 0)] * len(lead) + [(0, gap)])
        parts.append(piece.reshape(lead + (rows, LANES)))
    total = sum(part.shape[-2] for part in parts)
    gap = -total % SUBLANES
    if gap:
        parts.append(jnp.zeros(lead + (gap, LANES), parts[0].dtype))
    return jnp.concatenate(parts, axis=-2)


def local(
    grid, latents, conditioning, counts, cotangent, ada_weights, attn_weights, mlp_weights, flat_biases
):
    slot_count, length, model_width = latents.shape
    shards = (ada_weights, attn_weights, mlp_weights, flat_biases)
    gathered = gather_all(grid, pack(shards, ()))
    gathered = gathered.reshape((grid.count,) + gathered.shape[-2:])
    flats, row = [], 0
    for shard in shards:
        extent = shard.shape[0]
        rows = padded_rows(extent)
        flats.append(
            gathered[:, row : row + rows].reshape(grid.count, rows * LANES)[:, :extent].reshape(-1)
        )
        row += rows
    weights = unpack(flats[0], flats[1], flats[2], flats[3], model_width, FF)
    live = jnp.arange(slot_count, dtype=jnp.int32) < counts[0]
    output, saved = forward_group(latents, conditioning, live, weights, HEADS)
    grad_after, mod_tail, mlp_terms = mlp_backward(saved, cotangent, live, weights)
    grad_latents, grad_conditioning, attn_terms = attention_backward(
        saved, conditioning, grad_after, mod_tail, weights, HEADS
    )

    def flat(*terms):
        return jnp.concatenate(
            [term.astype(jnp.bfloat16).reshape(-1) for term in terms]
        ).reshape(grid.count, -1)

    packed = pack(
        [
            flat(attn_terms[0]),
            flat(attn_terms[1], attn_terms[2]),
            flat(mlp_terms[0], mlp_terms[1]),
            flat(attn_terms[3], attn_terms[4], attn_terms[5], attn_terms[6], mlp_terms[2], mlp_terms[3]),
        ],
        (grid.count,),
    )
    summed = scatter_sum(grid, packed.reshape(grid.sizes + packed.shape[1:]))
    grads, row = [], 0
    for shard in shards:
        extent = shard.shape[0]
        rows = padded_rows(extent)
        grads.append(summed[row : row + rows].reshape(-1)[:extent])
        row += rows
    return (output, grad_latents, grad_conditioning) + tuple(grads)


def solution(mesh):
    in_specs = (
        P(("dp", "fsdp"), None, None),
        P(("dp", "fsdp"), None),
        P(("dp", "fsdp")),
        P(("dp", "fsdp"), None, None),
        P(("dp", "fsdp")),
        P(("dp", "fsdp")),
        P(("dp", "fsdp")),
        P(("dp", "fsdp")),
    )
    out_specs = (
        P(("dp", "fsdp"), None, None),
        P(("dp", "fsdp"), None, None),
        P(("dp", "fsdp"), None),
        P(("dp", "fsdp")),
        P(("dp", "fsdp")),
        P(("dp", "fsdp")),
        P(("dp", "fsdp")),
    )
    return jax.shard_map(partial(local, Grid(mesh)), mesh=mesh, in_specs=in_specs, out_specs=out_specs, check_vma=False)
```

```python
from functools import partial
import math

import jax
import jax.numpy as jnp
from jax import lax
from jax.experimental import pallas as pl
from jax.experimental.pallas import tpu as pltpu
from jax.sharding import PartitionSpec as P

FF = 1536
HEADS = 6


EPSILON = 1e-06
GELU_COEF = 0.044715
ROOT_TWO_OVER_PI = 0.7978845608028654


def layer_norm(values):
    centre = values - jnp.mean(values, axis=-1, keepdims=True)
    inverse = lax.rsqrt(jnp.mean(centre * centre, axis=-1, keepdims=True) + EPSILON)
    return (centre * inverse, inverse)


def norm_backward(grad_norm, normed, inverse):
    first = jnp.mean(grad_norm, axis=-1, keepdims=True)
    second = jnp.mean(grad_norm * normed, axis=-1, keepdims=True)
    return (grad_norm - first - normed * second) * inverse


def gelu_value(pre_act):
    inner = ROOT_TWO_OVER_PI * (pre_act + GELU_COEF * pre_act * pre_act * pre_act)
    return 0.5 * pre_act * (1.0 + jnp.tanh(inner))


def gelu_slope(pre_act):
    tanh_part = jnp.tanh(ROOT_TWO_OVER_PI * (pre_act + GELU_COEF * pre_act * pre_act * pre_act))
    return 0.5 * (1.0 + tanh_part) + 0.5 * pre_act * (
        1.0 - tanh_part * tanh_part
    ) * ROOT_TWO_OVER_PI * (1.0 + 3.0 * GELU_COEF * pre_act * pre_act)


def silu_slope(values):
    sigma = jax.nn.sigmoid(values)
    return sigma * (1.0 + values * (1.0 - sigma))


def unpack(ada_flat, attn_flat, mlp_flat, bias_flat, model_width, hidden_units):
    qkv_size = 3 * model_width * model_width
    fc1_size = model_width * hidden_units
    pieces = [
        ada_flat.reshape(model_width, 6 * model_width),
        attn_flat[:qkv_size].reshape(model_width, 3 * model_width),
        attn_flat[qkv_size:].reshape(model_width, model_width),
        mlp_flat[:fc1_size].reshape(model_width, hidden_units),
        mlp_flat[fc1_size:].reshape(hidden_units, model_width),
    ]
    offset = 0
    for extent_now in [
        6 * model_width,
        model_width,
        model_width,
        model_width,
        hidden_units,
        model_width,
    ]:
        pieces.append(bias_flat[offset : offset + extent_now])
        offset = offset + extent_now
    return tuple(pieces)


LANES = 128
SUBLANES = 16
AXES = ("dp", "fsdp")
MESH = pl.DeviceIdType.MESH


class Grid:
    def __init__(self, mesh):
        dp, fsdp = mesh.shape["dp"], mesh.shape["fsdp"]
        side = math.isqrt(dp)
        self.high = side if side * side == dp else 1
        self.low = dp // self.high
        self.pair = 2 if fsdp % 2 == 0 else 1
        self.depth = fsdp // self.pair
        self.count = dp * fsdp
        self.sizes = (self.high, self.low, self.depth, self.pair)

    def here(self):
        a, f = lax.axis_index("dp"), lax.axis_index("fsdp")
        return [a // self.low, a % self.low, f // self.pair, f % self.pair]

    def peer(self, here, axis, step):
        spot = list(here)
        spot[axis] = lax.rem(here[axis] + step, self.sizes[axis])
        return spot

    def ident(self, spot):
        return (spot[0] * self.low + spot[1], spot[2] * self.pair + spot[3])

    def barrier(self, here):
        sem = pltpu.get_barrier_semaphore()
        total = 0
        for axis in range(4):
            for step in range(1, self.sizes[axis]):
                pl.semaphore_signal(
                    sem, inc=1, device_id=self.ident(self.peer(here, axis, step)), device_id_type=MESH
                )
                total += 1
        pl.semaphore_wait(sem, total)


def split_rows(rows, parts):
    units = rows // SUBLANES
    parts = min(parts, units)
    cuts = [units * k // parts for k in range(parts + 1)]
    return [(cuts[k] * SUBLANES, (cuts[k + 1] - cuts[k]) * SUBLANES) for k in range(parts)]


def gather_kernel(grid, chunks, in_ref, out_ref, send_sem, recv_sem, own_sem):
    here = grid.here()
    hi, lo, z, c = here
    spare = iter(range(send_sem.shape[0]))
    grid.barrier(here)

    def push(src, dst, spot):
        k = next(spare)
        copy = pltpu.make_async_remote_copy(
            src_ref=src, dst_ref=dst, send_sem=send_sem.at[k], recv_sem=recv_sem.at[k],
            device_id=grid.ident(spot), device_id_type=MESH,
        )
        copy.start()
        return copy

    def steps(axis):
        return [grid.peer(here, axis, s) for s in range(1, grid.sizes[axis])]

    everything = []

    def pushes(src, dst, spots):
        copies = [push(src, dst, spot) for spot in spots]
        everything.extend(copies)
        return copies

    def arrive(copies):
        for copy in copies:
            copy.wait_recv()

    own = pltpu.make_async_copy(in_ref, out_ref.at[hi, lo, z, c], own_sem)
    own.start()
    along_z, first, second, swap = [], [], [], []
    for start, size in chunks:
        rows = pl.ds(start, size)
        along_z.append(pushes(in_ref.at[rows], out_ref.at[hi, lo, z, c, rows], steps(2)))
    own.wait()
    for k, (start, size) in enumerate(chunks):
        rows = pl.ds(start, size)
        arrive(along_z[k])
        part = out_ref.at[hi, lo, :, c, rows]
        first.append(pushes(part, part, steps(1 if k % 2 == 0 else 0)))
        swap += pushes(part, part, steps(3))
    for k, (start, size) in enumerate(chunks):
        rows = pl.ds(start, size)
        arrive(first[k])
        if k % 2 == 0:
            part = out_ref.at[hi, :, :, c, rows]
            second.append(pushes(part, part, steps(0)))
            others = [out_ref.at[hi, spot[1], :, c, rows] for spot in steps(1)]
        else:
            part = out_ref.at[:, lo, :, c, rows]
            second.append(pushes(part, part, steps(1)))
            others = [out_ref.at[spot[0], lo, :, c, rows] for spot in steps(0)]
        for other in others:
            swap += pushes(other, other, steps(3))
    for k, (start, size) in enumerate(chunks):
        rows = pl.ds(start, size)
        arrive(second[k])
        if k % 2 == 0:
            others = [out_ref.at[spot[0], :, :, c, rows] for spot in steps(0)]
        else:
            others = [out_ref.at[:, spot[1], :, c, rows] for spot in steps(1)]
        for other in others:
            swap += pushes(other, other, steps(3))
    arrive(swap)
    for copy in everything:
        copy.wait_send()


def gather_copies(grid, chunk_count):
    high, low, depth, pair = grid.sizes
    first = lambda k: low - 1 if k % 2 == 0 else high - 1
    second = lambda k: high - 1 if k % 2 == 0 else low - 1
    return sum(
        (depth - 1) + first(k) + second(k) + (pair - 1) * (1 + first(k) + second(k))
        for k in range(chunk_count)
    )


def gather_all(grid, slab):
    rows = slab.shape[0]
    chunks = split_rows(rows, 4)
    copies = gather_copies(grid, len(chunks))
    return pl.pallas_call(
        partial(gather_kernel, grid, chunks),
        out_shape=jax.ShapeDtypeStruct(grid.sizes + slab.shape, slab.dtype),
        in_specs=[pl.BlockSpec(memory_space=pltpu.VMEM)],
        out_specs=pl.BlockSpec(memory_space=pltpu.VMEM),
        scratch_shapes=[
            pltpu.SemaphoreType.DMA((copies,)),
            pltpu.SemaphoreType.DMA((copies,)),
            pltpu.SemaphoreType.DMA,
        ],
        compiler_params=pltpu.CompilerParams(
            collective_id=0, has_side_effects=True, vmem_limit_bytes=48 * 1024 * 1024
        ),
    )(slab)


def scatter_kernel(grid, chunks, arrays, *refs):
    g_refs, refs = refs[:arrays], refs[arrays:]
    out_refs, refs = refs[:arrays], refs[arrays:]
    pair_bufs, refs = refs[:arrays], refs[arrays:]
    accs, refs = refs[:arrays], refs[arrays:]
    one_bufs, refs = refs[:arrays], refs[arrays:]
    two_bufs, refs = refs[:arrays], refs[arrays:]
    z_bufs, (send_sem, recv_sem) = refs[:arrays], refs[arrays:]
    here = grid.here()
    hi, lo, z, c = here
    spare = iter(range(send_sem.shape[0]))
    grid.barrier(here)
    everything = []

    def push(src, dst, spot):
        k = next(spare)
        copy = pltpu.make_async_remote_copy(
            src_ref=src, dst_ref=dst, send_sem=send_sem.at[k], recv_sem=recv_sem.at[k],
            device_id=grid.ident(spot), device_id_type=MESH,
        )
        copy.start()
        everything.append(copy)
        return copy

    def steps(axis):
        return [(s - 1, grid.peer(here, axis, s)) for s in range(1, grid.sizes[axis])]

    def arrive(copies):
        for copy in copies:
            copy.wait_recv()

    def add(into, terms, first, second):
        def body(t, _):
            i, j = t // second, t % second
            total = terms[0](i, j)[...].astype(jnp.float32)
            for term in terms[1:]:
                total = total + term(i, j)[...].astype(jnp.float32)
            target = into(i, j)
            target[...] = total.astype(target.dtype)
            return 0

        lax.fori_loop(0, first * second, body, 0)

    high, low, depth, pair = grid.sizes
    swaps, ones, twos, lines = [], [], [], []
    for n, start, size in chunks:
        rows = pl.ds(start, size)
        g_ref, pair_buf = g_refs[n], pair_bufs[n]
        swaps.append(
            [push(g_ref.at[:, :, :, spot[3], rows], pair_buf.at[:, :, :, rows], spot) for _, spot in steps(3)]
        )
    for k, (n, start, size) in enumerate(chunks):
        rows = pl.ds(start, size)
        g_ref, pair_buf, acc, buf_one = g_refs[n], pair_bufs[n], accs[n], one_bufs[n]
        arrive(swaps[k])
        terms = [lambda i, j: g_ref.at[i // low, i % low, j, c, rows]]
        if pair > 1:
            terms.append(lambda i, j: pair_buf.at[i // low, i % low, j, rows])
        add(lambda i, j: acc.at[i // low, i % low, j, rows], terms, high * low, depth)
        if k % 2 == 0:
            ones.append(
                [push(acc.at[spot[0], :, :, rows], buf_one.at[s, 0:low, :, rows], spot) for s, spot in steps(0)]
            )
        else:
            ones.append(
                [push(acc.at[:, spot[1], :, rows], buf_one.at[s, 0:high, :, rows], spot) for s, spot in steps(1)]
            )
    for k, (n, start, size) in enumerate(chunks):
        rows = pl.ds(start, size)
        acc, buf_one, buf_two = accs[n], one_bufs[n], two_bufs[n]
        arrive(ones[k])
        even = k % 2 == 0
        mine = (lambda i, j: acc.at[hi, i, j, rows]) if even else (lambda i, j: acc.at[i, lo, j, rows])
        terms = [mine] + [
            (lambda i, j, s=s: buf_one.at[s, i, j, rows]) for s, _ in steps(0 if even else 1)
        ]
        add(mine, terms, low if even else high, depth)
        if even:
            twos.append(
                [push(acc.at[hi, spot[1], :, rows], buf_two.at[s, :, rows], spot) for s, spot in steps(1)]
            )
        else:
            twos.append(
                [push(acc.at[spot[0], lo, :, rows], buf_two.at[s, :, rows], spot) for s, spot in steps(0)]
            )
    for k, (n, start, size) in enumerate(chunks):
        rows = pl.ds(start, size)
        acc, buf_two, buf_z = accs[n], two_bufs[n], z_bufs[n]
        arrive(twos[k])
        mine = lambda i, j: acc.at[hi, lo, j, rows]
        terms = [mine] + [
            (lambda i, j, s=s: buf_two.at[s, j, rows]) for s, _ in steps(1 if k % 2 == 0 else 0)
        ]
        add(mine, terms, 1, depth)
        lines.append(
            [push(acc.at[hi, lo, spot[2], rows], buf_z.at[s, rows], spot) for s, spot in steps(2)]
        )
    for k, (n, start, size) in enumerate(chunks):
        rows = pl.ds(start, size)
        acc, buf_z = accs[n], z_bufs[n]
        arrive(lines[k])
        total = acc[hi, lo, z, rows].astype(jnp.float32)
        for s in range(depth - 1):
            total = total + buf_z[s, rows].astype(jnp.float32)
        out_refs[n][rows, :] = total
    for copy in everything:
        copy.wait_send()


def scatter_sum(grid, arrays):
    high, low, depth, pair = grid.sizes
    chunks = []
    for n, array in enumerate(arrays):
        rows = array.shape[-2]
        if rows % (2 * SUBLANES) == 0:
            chunks += [(n, 0, rows // 2), (n, rows // 2, rows // 2)]
        else:
            chunks.append((n, 0, rows))
    copies = len(chunks) * (high + low + depth + pair - 4)
    kind = arrays[0].dtype
    tails = [array.shape[-2:] for array in arrays]
    side = max(high, low)
    shapes = [
        (high, low, depth), (high, low, depth), (max(side - 1, 1), side, depth),
        (max(side - 1, 1), depth), (max(depth - 1, 1),),
    ]
    return pl.pallas_call(
        partial(scatter_kernel, grid, chunks, len(arrays)),
        out_shape=[jax.ShapeDtypeStruct(tail, jnp.float32) for tail in tails],
        in_specs=[pl.BlockSpec(memory_space=pltpu.VMEM)] * len(arrays),
        out_specs=[pl.BlockSpec(memory_space=pltpu.VMEM)] * len(arrays),
        scratch_shapes=[pltpu.VMEM(shape + tail, kind) for shape in shapes for tail in tails]
        + [pltpu.SemaphoreType.DMA((copies,)), pltpu.SemaphoreType.DMA((copies,))],
        compiler_params=pltpu.CompilerParams(
            collective_id=1, has_side_effects=True, vmem_limit_bytes=48 * 1024 * 1024
        ),
    )(*arrays)


def padded_rows(extent):
    return -(-extent // LANES)


def pack(pieces, lead):
    parts = []
    for piece in pieces:
        extent = piece.shape[-1]
        rows = padded_rows(extent)
        gap = rows * LANES - extent
        if gap:
            piece = jnp.pad(piece, [(0, 0)] * len(lead) + [(0, gap)])
        parts.append(piece.reshape(lead + (rows, LANES)))
    total = sum(part.shape[-2] for part in parts)
    gap = -total % SUBLANES
    if gap:
        parts.append(jnp.zeros(lead + (gap, LANES), parts[0].dtype))
    return jnp.concatenate(parts, axis=-2)


def dot(left, right, contract=(1, 0)):
    return lax.dot_general(
        left, right, (((contract[0],), (contract[1],)), ((), ())), preferred_element_type=jnp.float32
    )


def block_kernel(
    count_ref, x_ref, cond_ref, cot_ref, w_ada, w_qkv, w_proj, w_one, w_two, bias_ref,
    out_ref, gx_ref, gcond_ref, g_ada, g_qkv, g_proj, g_one, g_two, gbias_ref,
    mod, norm_one, inv_one, h_one, qkv, probs, mixed, branch, norm_two, inv_two, h_two,
    pre, act, mlp, wide, back, dx, small, dqkv, dmod,
):
    slots, length, width = x_ref.shape
    hidden = w_one.shape[1]
    rows_all = slots * length
    heads = probs.shape[1]
    head_dim = width // heads
    score_scale = head_dim ** (-0.5)
    f32, b16 = jnp.float32, jnp.bfloat16
    tile = 256 if hidden % 256 == 0 else hidden
    count = count_ref[0]
    o_query, o_value = 6 * width, 7 * width
    o_proj, o_one, o_two = 8 * width, 9 * width, 9 * width + hidden
    lane = lax.broadcasted_iota(jnp.int32, (length, 2 * head_dim), 1)
    lower = lane < head_dim

    def slot_loop(body):
        def step(s, _):
            body(s, pl.ds(pl.multiple_of(s * length, length), length))
            return 0

        lax.fori_loop(0, slots, step, 0)

    def part(s, k):
        return mod[pl.ds(s, 1), k * width : (k + 1) * width]

    def only(pair_block, first):
        return jnp.where(lower if first else jnp.logical_not(lower), pair_block, jnp.zeros_like(pair_block))

    def column_sum(values):
        return jnp.sum(values, axis=0, keepdims=True)

    cond = cond_ref[...]
    cond_act = (cond * jax.nn.sigmoid(cond)).astype(b16)
    mod[...] = dot(cond_act, w_ada[...]) + bias_ref[:, : 6 * width]

    def norm_first(s, rows):
        normed, inverse = layer_norm(x_ref[s])
        norm_one[rows, :] = normed
        inv_one[rows, :] = inverse
        h_one[rows, :] = (normed * (1.0 + part(s, 1)) + part(s, 0)).astype(b16)

    slot_loop(norm_first)
    for k, offset in enumerate((o_query, None, o_value)):
        cols = slice(k * width, (k + 1) * width)
        value = dot(h_one[...], w_qkv[:, cols])
        if offset is not None:
            value = value + bias_ref[:, offset : offset + width]
        qkv[:, cols] = value.astype(b16)

    def attend(s, rows):
        for pair in range(heads // 2):
            at = pair * 2 * head_dim
            query = qkv[rows, at : at + 2 * head_dim]
            key = qkv[rows, width + at : width + at + 2 * head_dim]
            value = qkv[rows, 2 * width + at : 2 * width + at + 2 * head_dim]
            halves = []
            for h in range(2):
                scores = dot(only(query, h == 0), key, (1, 1)) * score_scale
                total = jnp.log(jnp.sum(jnp.exp(scores), axis=-1, keepdims=True))
                prob = jnp.exp(scores - total)
                probs[s, 2 * pair + h] = prob
                halves.append(dot(prob.astype(b16), value))
            mixed[rows, at : at + 2 * head_dim] = jnp.where(lower, halves[0], halves[1]).astype(b16)

    slot_loop(attend)
    branch[...] = dot(mixed[...], w_proj[...]) + bias_ref[:, o_proj : o_proj + width]

    def norm_second(s, rows):
        after = x_ref[s] + part(s, 2) * branch[rows, :]
        dx[rows, :] = after
        normed, inverse = layer_norm(after)
        norm_two[rows, :] = normed
        inv_two[rows, :] = inverse
        h_two[rows, :] = (normed * (1.0 + part(s, 4)) + part(s, 3)).astype(b16)

    slot_loop(norm_second)

    def up(t, _):
        cols = pl.ds(pl.multiple_of(t * tile, tile), tile)
        shift = bias_ref[:, pl.ds(pl.multiple_of(o_one + t * tile, LANES), tile)]
        value = dot(h_two[...], w_one[:, cols]) + shift
        pre[:, cols] = value
        act[:, cols] = gelu_value(value).astype(b16)
        return 0

    lax.fori_loop(0, hidden // tile, up, 0)
    mlp[...] = dot(act[...], w_two[...]) + bias_ref[:, o_two : o_two + width]

    gbias_ref[...] = jnp.zeros_like(gbias_ref)

    def finish(s, rows):
        live = s < count
        value = mlp[rows, :]
        out_ref[s] = jnp.where(live, dx[rows, :] + part(s, 5) * value, 0.0)
        grad = jnp.where(live, cot_ref[s], 0.0)
        dmod[pl.ds(s, 1), 5 * width :] = column_sum(grad * value)
        full = grad * part(s, 5)
        gbias_ref[:, o_two : o_two + width] += column_sum(full)
        small[rows, :] = full.astype(b16)

    slot_loop(finish)

    def down(t, _):
        cols = pl.ds(pl.multiple_of(t * tile, tile), tile)
        full = dot(small[...], w_two[cols, :], (1, 1)) * gelu_slope(pre[:, cols])
        gbias_ref[:, pl.ds(pl.multiple_of(o_one + t * tile, LANES), tile)] = column_sum(full)
        grad = full.astype(b16)
        wide[:, cols] = grad
        g_two[cols, :] = dot(act[:, cols], small[...], (0, 0)).astype(g_two.dtype)
        g_one[:, cols] = dot(h_two[...], grad, (0, 0)).astype(g_one.dtype)
        return 0

    lax.fori_loop(0, hidden // tile, down, 0)
    back[...] = dot(wide[...], w_one[...], (1, 1))

    def mlp_back(s, rows):
        grad_two = back[rows, :]
        normed = norm_two[rows, :]
        dmod[pl.ds(s, 1), 4 * width : 5 * width] = column_sum(grad_two * normed)
        dmod[pl.ds(s, 1), 3 * width : 4 * width] = column_sum(grad_two)
        after = jnp.where(s < count, cot_ref[s], 0.0) + norm_backward(
            grad_two * (1.0 + part(s, 4)), normed, inv_two[rows, :]
        )
        dx[rows, :] = after
        dmod[pl.ds(s, 1), 2 * width : 3 * width] = column_sum(after * branch[rows, :])
        full = after * part(s, 2)
        gbias_ref[:, o_proj : o_proj + width] += column_sum(full)
        small[rows, :] = full.astype(b16)

    slot_loop(mlp_back)
    g_proj[...] = dot(mixed[...], small[...], (0, 0)).astype(g_proj.dtype)
    mixed[...] = dot(small[...], w_proj[...], (1, 1)).astype(b16)

    def attend_back(s, rows):
        for pair in range(heads // 2):
            at = pair * 2 * head_dim
            span = slice(at, at + 2 * head_dim)
            query = qkv[rows, span]
            key = qkv[rows, width + at : width + at + 2 * head_dim]
            value = qkv[rows, 2 * width + at : 2 * width + at + 2 * head_dim]
            grad = mixed[rows, span]
            d_query, d_key, d_value = [], [], []
            for h in range(2):
                prob = probs[s, 2 * pair + h]
                d_prob = dot(only(grad, h == 0), value, (1, 1))
                d_value.append(dot(prob.astype(b16), grad, (0, 0)))
                delta = jnp.sum(prob * d_prob, axis=-1, keepdims=True)
                d_score = (prob * (d_prob - delta) * score_scale).astype(b16)
                d_query.append(dot(d_score, key))
                d_key.append(dot(d_score, query, (0, 0)))
            d_query = jnp.where(lower, d_query[0], d_query[1]).astype(b16)
            d_key = jnp.where(lower, d_key[0], d_key[1]).astype(b16)
            d_value = jnp.where(lower, d_value[0], d_value[1]).astype(b16)
            dqkv[rows, span] = d_query
            dqkv[rows, width + at : width + at + 2 * head_dim] = d_key
            dqkv[rows, 2 * width + at : 2 * width + at + 2 * head_dim] = d_value
            gbias_ref[:, o_query + at : o_query + at + 2 * head_dim] += column_sum(d_query.astype(f32))
            gbias_ref[:, o_value + at : o_value + at + 2 * head_dim] += column_sum(d_value.astype(f32))

    slot_loop(attend_back)
    for k in range(3):
        cols = slice(k * width, (k + 1) * width)
        g_qkv[:, cols] = dot(h_one[...], dqkv[:, cols], (0, 0)).astype(g_qkv.dtype)
    back[...] = dot(dqkv[...], w_qkv[...], (1, 1))

    def attn_back(s, rows):
        grad_one = back[rows, :]
        normed = norm_one[rows, :]
        dmod[pl.ds(s, 1), width : 2 * width] = column_sum(grad_one * normed)
        dmod[pl.ds(s, 1), :width] = column_sum(grad_one)
        gx_ref[s] = dx[rows, :] + norm_backward(
            grad_one * (1.0 + part(s, 1)), normed, inv_one[rows, :]
        )

    slot_loop(attn_back)
    gbias_ref[:, : 6 * width] = column_sum(dmod[...])
    grad_mod = dmod[...].astype(b16)
    g_ada[...] = dot(cond_act, grad_mod, (0, 0)).astype(g_ada.dtype)
    gcond_ref[...] = dot(grad_mod, w_ada[...], (1, 1)) * silu_slope(cond)


def run_block(counts, latents, conditioning, cotangent, weights, biases):
    slots, length, width = latents.shape
    w_ada, w_qkv, w_proj, w_one, w_two = weights
    hidden = w_one.shape[1]
    rows = slots * length
    f32, b16 = jnp.float32, jnp.bfloat16
    outs = [
        (latents.shape, f32), (latents.shape, f32), (conditioning.shape, f32),
        (w_ada.shape, b16), (w_qkv.shape, b16), (w_proj.shape, b16), (w_one.shape, b16),
        (w_two.shape, b16), (biases.shape, f32),
    ]
    scratch = [
        ((slots, 6 * width), f32), ((rows, width), f32), ((rows, 1), f32), ((rows, width), b16),
        ((rows, 3 * width), b16), ((slots, HEADS, length, length), f32), ((rows, width), b16),
        ((rows, width), f32), ((rows, width), f32), ((rows, 1), f32), ((rows, width), b16),
        ((rows, hidden), f32), ((rows, hidden), b16), ((rows, width), f32), ((rows, hidden), b16),
        ((rows, width), f32), ((rows, width), f32), ((rows, width), b16), ((rows, 3 * width), b16),
        ((slots, 6 * width), f32),
    ]
    vmem = pl.BlockSpec(memory_space=pltpu.VMEM)
    return pl.pallas_call(
        block_kernel,
        out_shape=[jax.ShapeDtypeStruct(shape, kind) for shape, kind in outs],
        in_specs=[pl.BlockSpec(memory_space=pltpu.SMEM)] + [vmem] * 9,
        out_specs=[vmem] * len(outs),
        scratch_shapes=[pltpu.VMEM(shape, kind) for shape, kind in scratch],
        compiler_params=pltpu.CompilerParams(vmem_limit_bytes=60 * 1024 * 1024),
    )(counts, latents, conditioning, cotangent, *weights, biases)


def local(
    grid, latents, conditioning, counts, cotangent, ada_weights, attn_weights, mlp_weights, flat_biases
):
    model_width = latents.shape[-1]
    shards = (ada_weights, attn_weights, mlp_weights, flat_biases)
    gathered = gather_all(grid, pack(shards, ()))
    gathered = gathered.reshape((grid.count,) + gathered.shape[-2:])
    flats, row = [], 0
    for shard in shards:
        extent = shard.shape[0]
        rows = padded_rows(extent)
        flats.append(
            gathered[:, row : row + rows].reshape(grid.count, rows * LANES)[:, :extent].reshape(-1)
        )
        row += rows
    weights = unpack(flats[0], flats[1], flats[2], flats[3], model_width, FF)[:5]
    biases = flats[3].astype(jnp.float32)[None]
    output, grad_latents, grad_conditioning, g_ada, g_qkv, g_proj, g_one, g_two, g_bias = run_block(
        counts, latents, conditioning, cotangent, weights, biases
    )

    def lines(flat, extent):
        rows = padded_rows(extent)
        flat = flat.reshape(grid.count, extent)
        if rows * LANES != extent:
            flat = jnp.pad(flat, ((0, 0), (0, rows * LANES - extent)))
        return flat.reshape(grid.sizes + (rows, LANES))

    flat_grads = [
        g_ada.reshape(-1),
        jnp.concatenate([g_qkv.reshape(-1), g_proj.reshape(-1)]),
        jnp.concatenate([g_one.reshape(-1), g_two.reshape(-1)]),
        g_bias.astype(jnp.bfloat16).reshape(-1),
    ]
    sums = scatter_sum(grid, [lines(flat, shard.shape[0]) for flat, shard in zip(flat_grads, shards)])
    grads = tuple(total.reshape(-1)[: shard.shape[0]] for total, shard in zip(sums, shards))
    return (output, grad_latents, grad_conditioning) + grads


def solution(mesh):
    in_specs = (
        P(("dp", "fsdp"), None, None),
        P(("dp", "fsdp"), None),
        P(("dp", "fsdp")),
        P(("dp", "fsdp"), None, None),
        P(("dp", "fsdp")),
        P(("dp", "fsdp")),
        P(("dp", "fsdp")),
        P(("dp", "fsdp")),
    )
    out_specs = (
        P(("dp", "fsdp"), None, None),
        P(("dp", "fsdp"), None, None),
        P(("dp", "fsdp"), None),
        P(("dp", "fsdp")),
        P(("dp", "fsdp")),
        P(("dp", "fsdp")),
        P(("dp", "fsdp")),
    )
    return jax.shard_map(partial(local, Grid(mesh)), mesh=mesh, in_specs=in_specs, out_specs=out_specs, check_vma=False)
```

```python
from functools import partial
import math

import jax
import jax.numpy as jnp
from jax import lax
from jax.experimental import pallas as pl
from jax.experimental.pallas import tpu as pltpu
from jax.sharding import PartitionSpec as P

FF = 1536
HEADS = 6


EPSILON = 1e-06
GELU_COEF = 0.044715
ROOT_TWO_OVER_PI = 0.7978845608028654


def layer_norm(values):
    centre = values - jnp.mean(values, axis=-1, keepdims=True)
    inverse = lax.rsqrt(jnp.mean(centre * centre, axis=-1, keepdims=True) + EPSILON)
    return (centre * inverse, inverse)


def norm_backward(grad_norm, normed, inverse):
    first = jnp.mean(grad_norm, axis=-1, keepdims=True)
    second = jnp.mean(grad_norm * normed, axis=-1, keepdims=True)
    return (grad_norm - first - normed * second) * inverse


def gelu_value(pre_act):
    inner = ROOT_TWO_OVER_PI * (pre_act + GELU_COEF * pre_act * pre_act * pre_act)
    return 0.5 * pre_act * (1.0 + jnp.tanh(inner))


def gelu_slope(pre_act):
    tanh_part = jnp.tanh(ROOT_TWO_OVER_PI * (pre_act + GELU_COEF * pre_act * pre_act * pre_act))
    return 0.5 * (1.0 + tanh_part) + 0.5 * pre_act * (
        1.0 - tanh_part * tanh_part
    ) * ROOT_TWO_OVER_PI * (1.0 + 3.0 * GELU_COEF * pre_act * pre_act)


def silu_slope(values):
    sigma = jax.nn.sigmoid(values)
    return sigma * (1.0 + values * (1.0 - sigma))


def unpack(ada_flat, attn_flat, mlp_flat, bias_flat, model_width, hidden_units):
    qkv_size = 3 * model_width * model_width
    fc1_size = model_width * hidden_units
    pieces = [
        ada_flat.reshape(model_width, 6 * model_width),
        attn_flat[:qkv_size].reshape(model_width, 3 * model_width),
        attn_flat[qkv_size:].reshape(model_width, model_width),
        mlp_flat[:fc1_size].reshape(model_width, hidden_units),
        mlp_flat[fc1_size:].reshape(hidden_units, model_width),
    ]
    offset = 0
    for extent_now in [
        6 * model_width,
        model_width,
        model_width,
        model_width,
        hidden_units,
        model_width,
    ]:
        pieces.append(bias_flat[offset : offset + extent_now])
        offset = offset + extent_now
    return tuple(pieces)


LANES = 128
SUBLANES = 16
AXES = ("dp", "fsdp")
MESH = pl.DeviceIdType.MESH


class Grid:
    def __init__(self, mesh):
        dp, fsdp = mesh.shape["dp"], mesh.shape["fsdp"]
        side = math.isqrt(dp)
        self.high = side if side * side == dp else 1
        self.low = dp // self.high
        self.pair = 2 if fsdp % 2 == 0 else 1
        self.depth = fsdp // self.pair
        self.count = dp * fsdp
        self.sizes = (self.high, self.low, self.depth, self.pair)

    def here(self):
        a, f = lax.axis_index("dp"), lax.axis_index("fsdp")
        return [a // self.low, a % self.low, f // self.pair, f % self.pair]

    def peer(self, here, axis, step):
        spot = list(here)
        spot[axis] = lax.rem(here[axis] + step, self.sizes[axis])
        return spot

    def ident(self, spot):
        return (spot[0] * self.low + spot[1], spot[2] * self.pair + spot[3])

    def barrier(self, here):
        sem = pltpu.get_barrier_semaphore()
        total = 0
        for axis in range(4):
            for step in range(1, self.sizes[axis]):
                pl.semaphore_signal(
                    sem, inc=1, device_id=self.ident(self.peer(here, axis, step)), device_id_type=MESH
                )
                total += 1
        pl.semaphore_wait(sem, total)


def chunk_rows(arrays):
    chunks = []
    for n, array in enumerate(arrays):
        rows = array.shape[-2]
        if rows % (2 * SUBLANES) == 0:
            chunks += [(n, 0, rows // 2), (n, rows // 2, rows // 2)]
        else:
            chunks.append((n, 0, rows))
    return chunks


class Mover:
    def __init__(self, grid, send_sem, recv_sem):
        self.grid, self.here = grid, grid.here()
        self.send_sem, self.recv_sem = send_sem, recv_sem
        self.started = []

    def push(self, src, dst, spot):
        k = len(self.started)
        copy = pltpu.make_async_remote_copy(
            src_ref=src, dst_ref=dst, send_sem=self.send_sem.at[k], recv_sem=self.recv_sem.at[k],
            device_id=self.grid.ident(spot), device_id_type=MESH,
        )
        copy.start()
        self.started.append(copy)
        return copy

    def spots(self, axis):
        return [self.grid.peer(self.here, axis, s) for s in range(1, self.grid.sizes[axis])]

    def pushes(self, ref, axis):
        return [self.push(ref, ref, spot) for spot in self.spots(axis)]

    def drain(self):
        for copy in self.started:
            copy.wait_send()


def arrive(copies):
    for copy in copies:
        copy.wait_recv()


class Spread:
    def __init__(self, mover, in_ref, out_ref, rows, low_first):
        self.mover, self.in_ref, self.out_ref, self.rows = mover, in_ref, out_ref, rows
        self.low_first = low_first
        self.swap = []

    def begin(self):
        hi, lo, z, c = self.mover.here
        src, dst = self.in_ref.at[self.rows], self.out_ref.at[hi, lo, z, c, self.rows]
        self.pending = [self.mover.push(src, dst, spot) for spot in self.mover.spots(2)]

    def first(self):
        hi, lo, z, c = self.mover.here
        arrive(self.pending)
        part = self.out_ref.at[hi, lo, :, c, self.rows]
        self.pending = self.mover.pushes(part, 1 if self.low_first else 0)
        self.swap += self.mover.pushes(part, 3)

    def second(self):
        hi, lo, z, c = self.mover.here
        arrive(self.pending)
        out, rows = self.out_ref, self.rows
        if self.low_first:
            self.pending = self.mover.pushes(out.at[hi, :, :, c, rows], 0)
            others = [out.at[hi, spot[1], :, c, rows] for spot in self.mover.spots(1)]
        else:
            self.pending = self.mover.pushes(out.at[:, lo, :, c, rows], 1)
            others = [out.at[spot[0], lo, :, c, rows] for spot in self.mover.spots(0)]
        for other in others:
            self.swap += self.mover.pushes(other, 3)

    def third(self):
        hi, lo, z, c = self.mover.here
        arrive(self.pending)
        out, rows = self.out_ref, self.rows
        if self.low_first:
            others = [out.at[spot[0], :, :, c, rows] for spot in self.mover.spots(0)]
        else:
            others = [out.at[:, spot[1], :, c, rows] for spot in self.mover.spots(1)]
        for other in others:
            self.swap += self.mover.pushes(other, 3)

    def end(self):
        arrive(self.swap)

    @staticmethod
    def copies(grid):
        high, low, depth, pair = grid.sizes
        return depth - 1 + (high + low - 2) + (pair - 1) * (1 + high + low - 2)


def gather_kernel(grid, chunks, arrays, *refs):
    in_refs, out_refs = refs[:arrays], refs[arrays : 2 * arrays]
    send_sem, recv_sem, own_sem = refs[2 * arrays :]
    mover = Mover(grid, send_sem, recv_sem)
    hi, lo, z, c = mover.here
    grid.barrier(mover.here)
    own = [
        pltpu.make_async_copy(in_refs[n], out_refs[n].at[hi, lo, z, c], own_sem.at[n])
        for n in range(arrays)
    ]
    for copy in own:
        copy.start()
    spreads = [
        Spread(mover, in_refs[n], out_refs[n], pl.ds(start, size), k % 2 == 0)
        for k, (n, start, size) in enumerate(chunks)
    ]
    for spread in spreads:
        spread.begin()
    for copy in own:
        copy.wait()
    for spread in spreads:
        spread.first()
    for spread in spreads:
        spread.second()
    for spread in spreads:
        spread.third()
    for spread in spreads:
        spread.end()
    mover.drain()


def gather_all(grid, arrays):
    chunks = chunk_rows(arrays)
    copies = Spread.copies(grid) * len(chunks)
    vmem = pl.BlockSpec(memory_space=pltpu.VMEM)
    return pl.pallas_call(
        partial(gather_kernel, grid, chunks, len(arrays)),
        out_shape=[jax.ShapeDtypeStruct(grid.sizes + array.shape, array.dtype) for array in arrays],
        in_specs=[vmem] * len(arrays),
        out_specs=[vmem] * len(arrays),
        scratch_shapes=[
            pltpu.SemaphoreType.DMA((copies,)),
            pltpu.SemaphoreType.DMA((copies,)),
            pltpu.SemaphoreType.DMA((len(arrays),)),
        ],
        compiler_params=pltpu.CompilerParams(
            collective_id=0, has_side_effects=True, vmem_limit_bytes=48 * 1024 * 1024
        ),
    )(*arrays)


def scatter_kernel(grid, chunks, arrays, note_ref, *refs):
    g_refs, refs = refs[:arrays], refs[arrays:]
    note_out, refs = refs[0], refs[1:]
    out_refs, refs = refs[:arrays], refs[arrays:]
    pair_bufs, refs = refs[:arrays], refs[arrays:]
    accs, refs = refs[:arrays], refs[arrays:]
    one_bufs, refs = refs[:arrays], refs[arrays:]
    two_bufs, refs = refs[:arrays], refs[arrays:]
    z_bufs, (send_sem, recv_sem, own_sem) = refs[:arrays], refs[arrays:]
    mover = Mover(grid, send_sem, recv_sem)
    here, push = mover.here, mover.push
    hi, lo, z, c = here
    grid.barrier(here)
    own = pltpu.make_async_copy(note_ref, note_out.at[hi, lo, z, c], own_sem)
    own.start()
    note = Spread(mover, note_ref, note_out, pl.ds(0, note_ref.shape[0]), True)
    note.begin()

    def steps(axis):
        return [(s - 1, grid.peer(here, axis, s)) for s in range(1, grid.sizes[axis])]

    def add(into, terms, first, second):
        def body(t, _):
            i, j = t // second, t % second
            total = terms[0](i, j)[...].astype(jnp.float32)
            for term in terms[1:]:
                total = total + term(i, j)[...].astype(jnp.float32)
            target = into(i, j)
            target[...] = total.astype(target.dtype)
            return 0

        lax.fori_loop(0, first * second, body, 0)

    high, low, depth, pair = grid.sizes
    swaps, ones, twos, lines = [], [], [], []
    for n, start, size in chunks:
        rows = pl.ds(start, size)
        g_ref, pair_buf = g_refs[n], pair_bufs[n]
        swaps.append(
            [push(g_ref.at[:, :, :, spot[3], rows], pair_buf.at[:, :, :, rows], spot) for _, spot in steps(3)]
        )
    own.wait()
    note.first()
    for k, (n, start, size) in enumerate(chunks):
        rows = pl.ds(start, size)
        g_ref, pair_buf, acc, buf_one = g_refs[n], pair_bufs[n], accs[n], one_bufs[n]
        arrive(swaps[k])
        terms = [lambda i, j: g_ref.at[i // low, i % low, j, c, rows]]
        if pair > 1:
            terms.append(lambda i, j: pair_buf.at[i // low, i % low, j, rows])
        add(lambda i, j: acc.at[i // low, i % low, j, rows], terms, high * low, depth)
        if k % 2 == 0:
            ones.append(
                [push(acc.at[spot[0], :, :, rows], buf_one.at[s, 0:low, :, rows], spot) for s, spot in steps(0)]
            )
        else:
            ones.append(
                [push(acc.at[:, spot[1], :, rows], buf_one.at[s, 0:high, :, rows], spot) for s, spot in steps(1)]
            )
    note.second()
    for k, (n, start, size) in enumerate(chunks):
        rows = pl.ds(start, size)
        acc, buf_one, buf_two = accs[n], one_bufs[n], two_bufs[n]
        arrive(ones[k])
        even = k % 2 == 0
        mine = (lambda i, j: acc.at[hi, i, j, rows]) if even else (lambda i, j: acc.at[i, lo, j, rows])
        terms = [mine] + [
            (lambda i, j, s=s: buf_one.at[s, i, j, rows]) for s, _ in steps(0 if even else 1)
        ]
        add(mine, terms, low if even else high, depth)
        if even:
            twos.append(
                [push(acc.at[hi, spot[1], :, rows], buf_two.at[s, :, rows], spot) for s, spot in steps(1)]
            )
        else:
            twos.append(
                [push(acc.at[spot[0], lo, :, rows], buf_two.at[s, :, rows], spot) for s, spot in steps(0)]
            )
    note.third()
    for k, (n, start, size) in enumerate(chunks):
        rows = pl.ds(start, size)
        acc, buf_two, buf_z = accs[n], two_bufs[n], z_bufs[n]
        arrive(twos[k])
        mine = lambda i, j: acc.at[hi, lo, j, rows]
        terms = [mine] + [
            (lambda i, j, s=s: buf_two.at[s, j, rows]) for s, _ in steps(1 if k % 2 == 0 else 0)
        ]
        add(mine, terms, 1, depth)
        lines.append(
            [push(acc.at[hi, lo, spot[2], rows], buf_z.at[s, rows], spot) for s, spot in steps(2)]
        )
    for k, (n, start, size) in enumerate(chunks):
        rows = pl.ds(start, size)
        acc, buf_z = accs[n], z_bufs[n]
        arrive(lines[k])
        total = acc[hi, lo, z, rows].astype(jnp.float32)
        for s in range(depth - 1):
            total = total + buf_z[s, rows].astype(jnp.float32)
        out_refs[n][rows, :] = total
    note.end()
    mover.drain()


def scatter_sum(grid, arrays, note):
    high, low, depth, pair = grid.sizes
    chunks = chunk_rows(arrays)
    copies = len(chunks) * (high + low + depth + pair - 4) + Spread.copies(grid)
    kind = arrays[0].dtype
    tails = [array.shape[-2:] for array in arrays]
    side = max(high, low)
    shapes = [
        (high, low, depth), (high, low, depth), (max(side - 1, 1), side, depth),
        (max(side - 1, 1), depth), (max(depth - 1, 1),),
    ]
    vmem = pl.BlockSpec(memory_space=pltpu.VMEM)
    return pl.pallas_call(
        partial(scatter_kernel, grid, chunks, len(arrays)),
        out_shape=[jax.ShapeDtypeStruct(grid.sizes + note.shape, note.dtype)]
        + [jax.ShapeDtypeStruct(tail, jnp.float32) for tail in tails],
        in_specs=[vmem] * (1 + len(arrays)),
        out_specs=[vmem] * (1 + len(arrays)),
        scratch_shapes=[pltpu.VMEM(shape + tail, kind) for shape in shapes for tail in tails]
        + [pltpu.SemaphoreType.DMA((copies,)), pltpu.SemaphoreType.DMA((copies,)), pltpu.SemaphoreType.DMA],
        compiler_params=pltpu.CompilerParams(
            collective_id=1, has_side_effects=True, vmem_limit_bytes=48 * 1024 * 1024
        ),
    )(note, *arrays)


def padded_rows(extent):
    return -(-extent // LANES)


def pack(pieces, lead):
    parts = []
    for piece in pieces:
        extent = piece.shape[-1]
        rows = padded_rows(extent)
        gap = rows * LANES - extent
        if gap:
            piece = jnp.pad(piece, [(0, 0)] * len(lead) + [(0, gap)])
        parts.append(piece.reshape(lead + (rows, LANES)))
    if len(parts) == 1:
        return parts[0]
    return jnp.concatenate(parts, axis=-2)


def dot(left, right, contract=(1, 0)):
    return lax.dot_general(
        left, right, (((contract[0],), (contract[1],)), ((), ())), preferred_element_type=jnp.float32
    )


def block_kernel(
    count_ref, x_ref, cond_ref, cot_ref, w_ada, w_qkv, w_proj, w_one, w_two, bias_ref,
    out_ref, gx_ref, gcond_ref, act_ref, dmod_ref, g_qkv, g_proj, g_one, g_two, gbias_ref,
    mod, norm_one, inv_one, h_one, qkv, probs, mixed, branch, norm_two, inv_two, h_two,
    pre, act, mlp, wide, back, dx, small, dqkv, dmod,
):
    slots, length, width = x_ref.shape
    hidden = w_one.shape[1]
    rows_all = slots * length
    heads = probs.shape[1]
    head_dim = width // heads
    score_scale = head_dim ** (-0.5)
    f32, b16 = jnp.float32, jnp.bfloat16
    tile = 256 if hidden % 256 == 0 else hidden
    count = count_ref[0]
    o_query, o_value = 6 * width, 7 * width
    o_proj, o_one, o_two = 8 * width, 9 * width, 9 * width + hidden
    lane = lax.broadcasted_iota(jnp.int32, (length, 2 * head_dim), 1)
    lower = lane < head_dim

    def slot_loop(body):
        def step(s, _):
            body(s, pl.ds(pl.multiple_of(s * length, length), length))
            return 0

        lax.fori_loop(0, slots, step, 0)

    def part(s, k):
        return mod[pl.ds(s, 1), k * width : (k + 1) * width]

    def only(pair_block, first):
        return jnp.where(lower if first else jnp.logical_not(lower), pair_block, jnp.zeros_like(pair_block))

    def column_sum(values):
        return jnp.sum(values, axis=0, keepdims=True)

    cond = cond_ref[...]
    cond_act = (cond * jax.nn.sigmoid(cond)).astype(b16)
    mod[...] = dot(cond_act, w_ada[...]) + bias_ref[:, : 6 * width]

    def norm_first(s, rows):
        normed, inverse = layer_norm(x_ref[s])
        norm_one[rows, :] = normed
        inv_one[rows, :] = inverse
        h_one[rows, :] = (normed * (1.0 + part(s, 1)) + part(s, 0)).astype(b16)

    slot_loop(norm_first)
    for k, offset in enumerate((o_query, None, o_value)):
        cols = slice(k * width, (k + 1) * width)
        value = dot(h_one[...], w_qkv[:, cols])
        if offset is not None:
            value = value + bias_ref[:, offset : offset + width]
        qkv[:, cols] = value.astype(b16)

    def attend(s, rows):
        for pair in range(heads // 2):
            at = pair * 2 * head_dim
            query = qkv[rows, at : at + 2 * head_dim]
            key = qkv[rows, width + at : width + at + 2 * head_dim]
            value = qkv[rows, 2 * width + at : 2 * width + at + 2 * head_dim]
            halves = []
            for h in range(2):
                scores = dot(only(query, h == 0), key, (1, 1)) * score_scale
                total = jnp.log(jnp.sum(jnp.exp(scores), axis=-1, keepdims=True))
                prob = jnp.exp(scores - total)
                probs[s, 2 * pair + h] = prob
                halves.append(dot(prob.astype(b16), value))
            mixed[rows, at : at + 2 * head_dim] = jnp.where(lower, halves[0], halves[1]).astype(b16)

    slot_loop(attend)
    branch[...] = dot(mixed[...], w_proj[...]) + bias_ref[:, o_proj : o_proj + width]

    def norm_second(s, rows):
        after = x_ref[s] + part(s, 2) * branch[rows, :]
        dx[rows, :] = after
        normed, inverse = layer_norm(after)
        norm_two[rows, :] = normed
        inv_two[rows, :] = inverse
        h_two[rows, :] = (normed * (1.0 + part(s, 4)) + part(s, 3)).astype(b16)

    slot_loop(norm_second)

    def up(t, _):
        cols = pl.ds(pl.multiple_of(t * tile, tile), tile)
        shift = bias_ref[:, pl.ds(pl.multiple_of(o_one + t * tile, LANES), tile)]
        value = dot(h_two[...], w_one[:, cols]) + shift
        pre[:, cols] = value
        act[:, cols] = gelu_value(value).astype(b16)
        return 0

    lax.fori_loop(0, hidden // tile, up, 0)
    mlp[...] = dot(act[...], w_two[...]) + bias_ref[:, o_two : o_two + width]

    gbias_ref[...] = jnp.zeros_like(gbias_ref)

    def finish(s, rows):
        live = s < count
        value = mlp[rows, :]
        out_ref[s] = jnp.where(live, dx[rows, :] + part(s, 5) * value, 0.0)
        grad = jnp.where(live, cot_ref[s], 0.0)
        dmod[pl.ds(s, 1), 5 * width :] = column_sum(grad * value)
        full = grad * part(s, 5)
        gbias_ref[:, o_two : o_two + width] += column_sum(full)
        small[rows, :] = full.astype(b16)

    slot_loop(finish)

    def down(t, _):
        cols = pl.ds(pl.multiple_of(t * tile, tile), tile)
        full = dot(small[...], w_two[cols, :], (1, 1)) * gelu_slope(pre[:, cols])
        gbias_ref[:, pl.ds(pl.multiple_of(o_one + t * tile, LANES), tile)] = column_sum(full)
        grad = full.astype(b16)
        wide[:, cols] = grad
        g_two[cols, :] = dot(act[:, cols], small[...], (0, 0)).astype(g_two.dtype)
        g_one[:, cols] = dot(h_two[...], grad, (0, 0)).astype(g_one.dtype)
        return 0

    lax.fori_loop(0, hidden // tile, down, 0)
    back[...] = dot(wide[...], w_one[...], (1, 1))

    def mlp_back(s, rows):
        grad_two = back[rows, :]
        normed = norm_two[rows, :]
        dmod[pl.ds(s, 1), 4 * width : 5 * width] = column_sum(grad_two * normed)
        dmod[pl.ds(s, 1), 3 * width : 4 * width] = column_sum(grad_two)
        after = jnp.where(s < count, cot_ref[s], 0.0) + norm_backward(
            grad_two * (1.0 + part(s, 4)), normed, inv_two[rows, :]
        )
        dx[rows, :] = after
        dmod[pl.ds(s, 1), 2 * width : 3 * width] = column_sum(after * branch[rows, :])
        full = after * part(s, 2)
        gbias_ref[:, o_proj : o_proj + width] += column_sum(full)
        small[rows, :] = full.astype(b16)

    slot_loop(mlp_back)
    g_proj[...] = dot(mixed[...], small[...], (0, 0)).astype(g_proj.dtype)
    mixed[...] = dot(small[...], w_proj[...], (1, 1)).astype(b16)

    def attend_back(s, rows):
        for pair in range(heads // 2):
            at = pair * 2 * head_dim
            span = slice(at, at + 2 * head_dim)
            query = qkv[rows, span]
            key = qkv[rows, width + at : width + at + 2 * head_dim]
            value = qkv[rows, 2 * width + at : 2 * width + at + 2 * head_dim]
            grad = mixed[rows, span]
            d_query, d_key, d_value = [], [], []
            for h in range(2):
                prob = probs[s, 2 * pair + h]
                d_prob = dot(only(grad, h == 0), value, (1, 1))
                d_value.append(dot(prob.astype(b16), grad, (0, 0)))
                delta = jnp.sum(prob * d_prob, axis=-1, keepdims=True)
                d_score = (prob * (d_prob - delta) * score_scale).astype(b16)
                d_query.append(dot(d_score, key))
                d_key.append(dot(d_score, query, (0, 0)))
            d_query = jnp.where(lower, d_query[0], d_query[1]).astype(b16)
            d_key = jnp.where(lower, d_key[0], d_key[1]).astype(b16)
            d_value = jnp.where(lower, d_value[0], d_value[1]).astype(b16)
            dqkv[rows, span] = d_query
            dqkv[rows, width + at : width + at + 2 * head_dim] = d_key
            dqkv[rows, 2 * width + at : 2 * width + at + 2 * head_dim] = d_value
            gbias_ref[:, o_query + at : o_query + at + 2 * head_dim] += column_sum(d_query.astype(f32))
            gbias_ref[:, o_value + at : o_value + at + 2 * head_dim] += column_sum(d_value.astype(f32))

    slot_loop(attend_back)
    for k in range(3):
        cols = slice(k * width, (k + 1) * width)
        g_qkv[:, cols] = dot(h_one[...], dqkv[:, cols], (0, 0)).astype(g_qkv.dtype)
    back[...] = dot(dqkv[...], w_qkv[...], (1, 1))

    def attn_back(s, rows):
        grad_one = back[rows, :]
        normed = norm_one[rows, :]
        dmod[pl.ds(s, 1), width : 2 * width] = column_sum(grad_one * normed)
        dmod[pl.ds(s, 1), :width] = column_sum(grad_one)
        gx_ref[s] = dx[rows, :] + norm_backward(
            grad_one * (1.0 + part(s, 1)), normed, inv_one[rows, :]
        )

    slot_loop(attn_back)
    gbias_ref[:, : 6 * width] = column_sum(dmod[...])
    grad_mod = dmod[...].astype(b16)
    act_ref[...] = cond_act
    dmod_ref[...] = grad_mod
    gcond_ref[...] = dot(grad_mod, w_ada[...], (1, 1)) * silu_slope(cond)


def run_block(counts, latents, conditioning, cotangent, weights, biases):
    slots, length, width = latents.shape
    w_ada, w_qkv, w_proj, w_one, w_two = weights
    hidden = w_one.shape[1]
    rows = slots * length
    f32, b16 = jnp.float32, jnp.bfloat16
    outs = [
        (latents.shape, f32), (latents.shape, f32), (conditioning.shape, f32),
        (conditioning.shape, b16), ((slots, 6 * width), b16), (w_qkv.shape, b16), (w_proj.shape, b16), (w_one.shape, b16),
        (w_two.shape, b16), (biases.shape, f32),
    ]
    scratch = [
        ((slots, 6 * width), f32), ((rows, width), f32), ((rows, 1), f32), ((rows, width), b16),
        ((rows, 3 * width), b16), ((slots, HEADS, length, length), f32), ((rows, width), b16),
        ((rows, width), f32), ((rows, width), f32), ((rows, 1), f32), ((rows, width), b16),
        ((rows, hidden), f32), ((rows, hidden), b16), ((rows, width), f32), ((rows, hidden), b16),
        ((rows, width), f32), ((rows, width), f32), ((rows, width), b16), ((rows, 3 * width), b16),
        ((slots, 6 * width), f32),
    ]
    vmem = pl.BlockSpec(memory_space=pltpu.VMEM)
    return pl.pallas_call(
        block_kernel,
        out_shape=[jax.ShapeDtypeStruct(shape, kind) for shape, kind in outs],
        in_specs=[pl.BlockSpec(memory_space=pltpu.SMEM)] + [vmem] * 9,
        out_specs=[vmem] * len(outs),
        scratch_shapes=[pltpu.VMEM(shape, kind) for shape, kind in scratch],
        compiler_params=pltpu.CompilerParams(vmem_limit_bytes=60 * 1024 * 1024),
    )(counts, latents, conditioning, cotangent, *weights, biases)


def local(
    grid, latents, conditioning, counts, cotangent, ada_weights, attn_weights, mlp_weights, flat_biases
):
    model_width = latents.shape[-1]
    slots = latents.shape[0]
    shards = (ada_weights, attn_weights, mlp_weights, flat_biases)
    flats = [
        whole.reshape(grid.count, -1)[:, : shard.shape[0]].reshape(-1)
        for whole, shard in zip(gather_all(grid, [pack([shard], ()) for shard in shards]), shards)
    ]
    weights = unpack(flats[0], flats[1], flats[2], flats[3], model_width, FF)[:5]
    biases = flats[3].astype(jnp.float32)[None]
    output, grad_latents, grad_conditioning, cond_act, grad_mod, g_qkv, g_proj, g_one, g_two, g_bias = (
        run_block(counts, latents, conditioning, cotangent, weights, biases)
    )

    def lines(flat, extent):
        rows = padded_rows(extent)
        flat = flat.reshape(grid.count, extent)
        if rows * LANES != extent:
            flat = jnp.pad(flat, ((0, 0), (0, rows * LANES - extent)))
        return flat.reshape(grid.sizes + (rows, LANES))

    flat_grads = [
        jnp.concatenate([g_qkv.reshape(-1), g_proj.reshape(-1)]),
        jnp.concatenate([g_one.reshape(-1), g_two.reshape(-1)]),
        g_bias.astype(jnp.bfloat16).reshape(-1),
    ]
    note = pack([grad_mod.reshape(-1), cond_act.reshape(-1)], ())
    notes, *sums = scatter_sum(
        grid, [lines(flat, shard.shape[0]) for flat, shard in zip(flat_grads, shards[1:])], note
    )
    notes = notes.reshape((grid.count,) + note.shape)
    mod_rows, act_rows = grad_mod.size // LANES, cond_act.size // LANES
    all_mod = notes[:, :mod_rows].reshape(grid.count * slots, 6 * model_width)
    all_act = notes[:, mod_rows : mod_rows + act_rows].reshape(grid.count * slots, model_width)
    grads = [own_rows(all_act, all_mod, ada_weights.shape[0])]
    grads += [total.reshape(-1)[: shard.shape[0]] for total, shard in zip(sums, shards[1:])]
    return (output, grad_latents, grad_conditioning) + tuple(grads)


def own_rows(left, right, extent):
    wide = right.shape[1]
    start = lax.axis_index(AXES) * extent
    rows = min(-(-extent // wide) + (1 if extent % wide else 0), left.shape[1])
    top = jnp.minimum(start // wide, left.shape[1] - rows)
    part = lax.dynamic_slice_in_dim(left, top, rows, 1)
    whole = dot(part, right, (0, 0)).reshape(-1)
    if rows * wide == extent:
        return whole
    return lax.dynamic_slice_in_dim(whole, start - top * wide, extent, 0)


def solution(mesh):
    in_specs = (
        P(("dp", "fsdp"), None, None),
        P(("dp", "fsdp"), None),
        P(("dp", "fsdp")),
        P(("dp", "fsdp"), None, None),
        P(("dp", "fsdp")),
        P(("dp", "fsdp")),
        P(("dp", "fsdp")),
        P(("dp", "fsdp")),
    )
    out_specs = (
        P(("dp", "fsdp"), None, None),
        P(("dp", "fsdp"), None, None),
        P(("dp", "fsdp"), None),
        P(("dp", "fsdp")),
        P(("dp", "fsdp")),
        P(("dp", "fsdp")),
        P(("dp", "fsdp")),
    )
    return jax.shard_map(partial(local, Grid(mesh)), mesh=mesh, in_specs=in_specs, out_specs=out_specs, check_vma=False)
```

```python
from functools import partial
import math

import jax
import jax.numpy as jnp
from jax import lax
from jax.experimental import pallas as pl
from jax.experimental.pallas import tpu as pltpu
from jax.sharding import PartitionSpec as P

FF = 1536
HEADS = 6


EPSILON = 1e-06
GELU_COEF = 0.044715
ROOT_TWO_OVER_PI = 0.7978845608028654


def layer_norm(values):
    centre = values - jnp.mean(values, axis=-1, keepdims=True)
    inverse = lax.rsqrt(jnp.mean(centre * centre, axis=-1, keepdims=True) + EPSILON)
    return (centre * inverse, inverse)


def norm_backward(grad_norm, normed, inverse):
    first = jnp.mean(grad_norm, axis=-1, keepdims=True)
    second = jnp.mean(grad_norm * normed, axis=-1, keepdims=True)
    return (grad_norm - first - normed * second) * inverse


def gelu_value(pre_act):
    inner = ROOT_TWO_OVER_PI * (pre_act + GELU_COEF * pre_act * pre_act * pre_act)
    return 0.5 * pre_act * (1.0 + jnp.tanh(inner))


def gelu_slope(pre_act):
    tanh_part = jnp.tanh(ROOT_TWO_OVER_PI * (pre_act + GELU_COEF * pre_act * pre_act * pre_act))
    return 0.5 * (1.0 + tanh_part) + 0.5 * pre_act * (
        1.0 - tanh_part * tanh_part
    ) * ROOT_TWO_OVER_PI * (1.0 + 3.0 * GELU_COEF * pre_act * pre_act)


def silu_slope(values):
    sigma = jax.nn.sigmoid(values)
    return sigma * (1.0 + values * (1.0 - sigma))


LANES = 128
SUBLANES = 16
AXES = ("dp", "fsdp")
MESH = pl.DeviceIdType.MESH


class Grid:
    def __init__(self, mesh):
        dp, fsdp = mesh.shape["dp"], mesh.shape["fsdp"]
        side = math.isqrt(dp)
        self.high = side if side * side == dp else 1
        self.low = dp // self.high
        self.pair = 2 if fsdp % 2 == 0 else 1
        self.depth = fsdp // self.pair
        self.count = dp * fsdp
        self.sizes = (self.high, self.low, self.depth, self.pair)

    def here(self):
        a, f = lax.axis_index("dp"), lax.axis_index("fsdp")
        return [a // self.low, a % self.low, f // self.pair, f % self.pair]

    def peer(self, here, axis, step):
        spot = list(here)
        spot[axis] = lax.rem(here[axis] + step, self.sizes[axis])
        return spot

    def ident(self, spot):
        return (spot[0] * self.low + spot[1], spot[2] * self.pair + spot[3])

    def barrier(self, here):
        sem = pltpu.get_barrier_semaphore()
        total = 0
        for axis in range(4):
            for step in range(1, self.sizes[axis]):
                pl.semaphore_signal(
                    sem, inc=1, device_id=self.ident(self.peer(here, axis, step)), device_id_type=MESH
                )
                total += 1
        pl.semaphore_wait(sem, total)


def chunk_rows(arrays):
    chunks = []
    for n, array in enumerate(arrays):
        rows = array.shape[-2]
        if rows % (2 * SUBLANES) == 0:
            chunks += [(n, 0, rows // 2), (n, rows // 2, rows // 2)]
        else:
            chunks.append((n, 0, rows))
    return chunks


class Mover:
    def __init__(self, grid, send_sem, recv_sem):
        self.grid, self.here = grid, grid.here()
        self.send_sem, self.recv_sem = send_sem, recv_sem
        self.started = []

    def push(self, src, dst, spot):
        k = len(self.started)
        copy = pltpu.make_async_remote_copy(
            src_ref=src, dst_ref=dst, send_sem=self.send_sem.at[k], recv_sem=self.recv_sem.at[k],
            device_id=self.grid.ident(spot), device_id_type=MESH,
        )
        copy.start()
        self.started.append(copy)
        return copy

    def spots(self, axis):
        return [self.grid.peer(self.here, axis, s) for s in range(1, self.grid.sizes[axis])]

    def pushes(self, ref, axis):
        return [self.push(ref, ref, spot) for spot in self.spots(axis)]

    def drain(self):
        for copy in self.started:
            copy.wait_send()


def arrive(copies):
    for copy in copies:
        copy.wait_recv()


class Spread:
    def __init__(self, mover, in_ref, out_ref, rows, low_first):
        self.mover, self.in_ref, self.out_ref, self.rows = mover, in_ref, out_ref, rows
        self.low_first = low_first
        self.swap = []

    def begin(self):
        hi, lo, z, c = self.mover.here
        src, dst = self.in_ref.at[self.rows], self.out_ref.at[hi, lo, z, c, self.rows]
        self.pending = [self.mover.push(src, dst, spot) for spot in self.mover.spots(2)]

    def first(self):
        hi, lo, z, c = self.mover.here
        arrive(self.pending)
        part = self.out_ref.at[hi, lo, :, c, self.rows]
        self.pending = self.mover.pushes(part, 1 if self.low_first else 0)
        self.swap += self.mover.pushes(part, 3)

    def second(self):
        hi, lo, z, c = self.mover.here
        arrive(self.pending)
        out, rows = self.out_ref, self.rows
        if self.low_first:
            self.pending = self.mover.pushes(out.at[hi, :, :, c, rows], 0)
            others = [out.at[hi, spot[1], :, c, rows] for spot in self.mover.spots(1)]
        else:
            self.pending = self.mover.pushes(out.at[:, lo, :, c, rows], 1)
            others = [out.at[spot[0], lo, :, c, rows] for spot in self.mover.spots(0)]
        for other in others:
            self.swap += self.mover.pushes(other, 3)

    def third(self):
        hi, lo, z, c = self.mover.here
        arrive(self.pending)
        out, rows = self.out_ref, self.rows
        if self.low_first:
            others = [out.at[spot[0], :, :, c, rows] for spot in self.mover.spots(0)]
        else:
            others = [out.at[:, spot[1], :, c, rows] for spot in self.mover.spots(1)]
        for other in others:
            self.swap += self.mover.pushes(other, 3)

    def end(self):
        arrive(self.swap)

    @staticmethod
    def copies(grid):
        high, low, depth, pair = grid.sizes
        return depth - 1 + (high + low - 2) + (pair - 1) * (1 + high + low - 2)


def gather_kernel(grid, chunks, arrays, *refs):
    in_refs, out_refs = refs[:arrays], refs[arrays : 2 * arrays]
    send_sem, recv_sem, own_sem = refs[2 * arrays :]
    mover = Mover(grid, send_sem, recv_sem)
    hi, lo, z, c = mover.here
    grid.barrier(mover.here)
    own = [
        pltpu.make_async_copy(in_refs[n], out_refs[n].at[hi, lo, z, c], own_sem.at[n])
        for n in range(arrays)
    ]
    for copy in own:
        copy.start()
    spreads = [
        Spread(mover, in_refs[n], out_refs[n], pl.ds(start, size), k % 2 == 0)
        for k, (n, start, size) in enumerate(chunks)
    ]
    for spread in spreads:
        spread.begin()
    for copy in own:
        copy.wait()
    for spread in spreads:
        spread.first()
    for spread in spreads:
        spread.second()
    for spread in spreads:
        spread.third()
    for spread in spreads:
        spread.end()
    mover.drain()


def gather_all(grid, arrays):
    chunks = chunk_rows(arrays)
    copies = Spread.copies(grid) * len(chunks)
    vmem = pl.BlockSpec(memory_space=pltpu.VMEM)
    return pl.pallas_call(
        partial(gather_kernel, grid, chunks, len(arrays)),
        out_shape=[jax.ShapeDtypeStruct(grid.sizes + array.shape, array.dtype) for array in arrays],
        in_specs=[vmem] * len(arrays),
        out_specs=[vmem] * len(arrays),
        scratch_shapes=[
            pltpu.SemaphoreType.DMA((copies,)),
            pltpu.SemaphoreType.DMA((copies,)),
            pltpu.SemaphoreType.DMA((len(arrays),)),
        ],
        compiler_params=pltpu.CompilerParams(
            collective_id=0, has_side_effects=True, vmem_limit_bytes=48 * 1024 * 1024
        ),
    )(*arrays)


def scatter_kernel(grid, chunks, arrays, extra, *refs):
    note_refs, refs = refs[:extra], refs[extra:]
    g_refs, refs = refs[:arrays], refs[arrays:]
    note_outs, refs = refs[:extra], refs[extra:]
    out_refs, refs = refs[:arrays], refs[arrays:]
    pair_bufs, refs = refs[:arrays], refs[arrays:]
    accs, refs = refs[:arrays], refs[arrays:]
    one_bufs, refs = refs[:arrays], refs[arrays:]
    two_bufs, refs = refs[:arrays], refs[arrays:]
    z_bufs, (send_sem, recv_sem, own_sem) = refs[:arrays], refs[arrays:]
    mover = Mover(grid, send_sem, recv_sem)
    here, push = mover.here, mover.push
    hi, lo, z, c = here
    grid.barrier(here)
    owns = [
        pltpu.make_async_copy(note_refs[n], note_outs[n].at[hi, lo, z, c], own_sem.at[n])
        for n in range(extra)
    ]
    notes = [
        Spread(mover, note_refs[n], note_outs[n], pl.ds(0, note_refs[n].shape[0]), n % 2 == 0)
        for n in range(extra)
    ]
    for own, note in zip(owns, notes):
        own.start()
        note.begin()

    def steps(axis):
        return [(s - 1, grid.peer(here, axis, s)) for s in range(1, grid.sizes[axis])]

    def add(into, terms, first, second):
        def body(t, _):
            i, j = t // second, t % second
            total = terms[0](i, j)[...].astype(jnp.float32)
            for term in terms[1:]:
                total = total + term(i, j)[...].astype(jnp.float32)
            target = into(i, j)
            target[...] = total.astype(target.dtype)
            return 0

        lax.fori_loop(0, first * second, body, 0)

    high, low, depth, pair = grid.sizes
    swaps, ones, twos, lines = [], [], [], []
    for n, start, size in chunks:
        rows = pl.ds(start, size)
        g_ref, pair_buf = g_refs[n], pair_bufs[n]
        swaps.append(
            [push(g_ref.at[:, :, :, spot[3], rows], pair_buf.at[:, :, :, rows], spot) for _, spot in steps(3)]
        )
    for own, note in zip(owns, notes):
        own.wait()
        note.first()
    for k, (n, start, size) in enumerate(chunks):
        rows = pl.ds(start, size)
        g_ref, pair_buf, acc, buf_one = g_refs[n], pair_bufs[n], accs[n], one_bufs[n]
        arrive(swaps[k])
        terms = [lambda i, j: g_ref.at[i // low, i % low, j, c, rows]]
        if pair > 1:
            terms.append(lambda i, j: pair_buf.at[i // low, i % low, j, rows])
        add(lambda i, j: acc.at[i // low, i % low, j, rows], terms, high * low, depth)
        if k % 2 == 0:
            ones.append(
                [push(acc.at[spot[0], :, :, rows], buf_one.at[s, 0:low, :, rows], spot) for s, spot in steps(0)]
            )
        else:
            ones.append(
                [push(acc.at[:, spot[1], :, rows], buf_one.at[s, 0:high, :, rows], spot) for s, spot in steps(1)]
            )
    for note in notes:
        note.second()
    for k, (n, start, size) in enumerate(chunks):
        rows = pl.ds(start, size)
        acc, buf_one, buf_two = accs[n], one_bufs[n], two_bufs[n]
        arrive(ones[k])
        even = k % 2 == 0
        mine = (lambda i, j: acc.at[hi, i, j, rows]) if even else (lambda i, j: acc.at[i, lo, j, rows])
        terms = [mine] + [
            (lambda i, j, s=s: buf_one.at[s, i, j, rows]) for s, _ in steps(0 if even else 1)
        ]
        add(mine, terms, low if even else high, depth)
        if even:
            twos.append(
                [push(acc.at[hi, spot[1], :, rows], buf_two.at[s, :, rows], spot) for s, spot in steps(1)]
            )
        else:
            twos.append(
                [push(acc.at[spot[0], lo, :, rows], buf_two.at[s, :, rows], spot) for s, spot in steps(0)]
            )
    for note in notes:
        note.third()
    for k, (n, start, size) in enumerate(chunks):
        rows = pl.ds(start, size)
        acc, buf_two, buf_z = accs[n], two_bufs[n], z_bufs[n]
        arrive(twos[k])
        mine = lambda i, j: acc.at[hi, lo, j, rows]
        terms = [mine] + [
            (lambda i, j, s=s: buf_two.at[s, j, rows]) for s, _ in steps(1 if k % 2 == 0 else 0)
        ]
        add(mine, terms, 1, depth)
        lines.append(
            [push(acc.at[hi, lo, spot[2], rows], buf_z.at[s, rows], spot) for s, spot in steps(2)]
        )
    for k, (n, start, size) in enumerate(chunks):
        rows = pl.ds(start, size)
        acc, buf_z = accs[n], z_bufs[n]
        arrive(lines[k])
        total = acc[hi, lo, z, rows].astype(jnp.float32)
        for s in range(depth - 1):
            total = total + buf_z[s, rows].astype(jnp.float32)
        out_refs[n][rows, :] = total
    for note in notes:
        note.end()
    mover.drain()


def scatter_sum(grid, arrays, notes):
    high, low, depth, pair = grid.sizes
    chunks = chunk_rows(arrays)
    copies = len(chunks) * (high + low + depth + pair - 4) + Spread.copies(grid) * len(notes)
    kind = arrays[0].dtype
    tails = [array.shape[-2:] for array in arrays]
    side = max(high, low)
    shapes = [
        (high, low, depth), (high, low, depth), (max(side - 1, 1), side, depth),
        (max(side - 1, 1), depth), (max(depth - 1, 1),),
    ]
    vmem = pl.BlockSpec(memory_space=pltpu.VMEM)
    return pl.pallas_call(
        partial(scatter_kernel, grid, chunks, len(arrays), len(notes)),
        out_shape=[jax.ShapeDtypeStruct(grid.sizes + note.shape, note.dtype) for note in notes]
        + [jax.ShapeDtypeStruct(tail, jnp.float32) for tail in tails],
        in_specs=[vmem] * (len(notes) + len(arrays)),
        out_specs=[vmem] * (len(notes) + len(arrays)),
        scratch_shapes=[pltpu.VMEM(shape + tail, kind) for shape in shapes for tail in tails]
        + [pltpu.SemaphoreType.DMA((copies,)), pltpu.SemaphoreType.DMA((copies,)), pltpu.SemaphoreType.DMA((len(notes),))],
        compiler_params=pltpu.CompilerParams(
            collective_id=1, has_side_effects=True, vmem_limit_bytes=48 * 1024 * 1024
        ),
    )(*notes, *arrays)


def padded_rows(extent):
    return -(-extent // LANES)


def pack(pieces, lead):
    parts = []
    for piece in pieces:
        extent = piece.shape[-1]
        rows = padded_rows(extent)
        gap = rows * LANES - extent
        if gap:
            piece = jnp.pad(piece, [(0, 0)] * len(lead) + [(0, gap)])
        parts.append(piece.reshape(lead + (rows, LANES)))
    if len(parts) == 1:
        return parts[0]
    return jnp.concatenate(parts, axis=-2)


def dot(left, right, contract=(1, 0)):
    return lax.dot_general(
        left, right, (((contract[0],), (contract[1],)), ((), ())), preferred_element_type=jnp.float32
    )


def block_kernel(
    count_ref, x_ref, cond_ref, cot_ref, w_ada, attn_ref, mlp_ref, bias_ref,
    out_ref, gx_ref, gcond_ref, act_ref, dmod_ref, g_attn, g_mlp, gbias_ref,
    line, w_qkv, w_proj, w_one, w_two, g_qkv, g_proj, g_one, g_two,
    mod, norm_one, inv_one, h_one, qkv, probs, mixed, branch, norm_two, inv_two, h_two,
    pre, act, mlp, wide, back, dx, small, dqkv, dmod,
):
    slots, length, width = x_ref.shape
    hidden = w_one.shape[1]
    rows_all = slots * length
    heads = probs.shape[1]
    head_dim = width // heads
    score_scale = head_dim ** (-0.5)
    f32, b16 = jnp.float32, jnp.bfloat16
    tile = 256 if hidden % 256 == 0 else hidden
    count = count_ref[0]
    o_query, o_value = 6 * width, 7 * width
    o_proj, o_one, o_two = 8 * width, 9 * width, 9 * width + hidden
    lane = lax.broadcasted_iota(jnp.int32, (length, 2 * head_dim), 1)
    lower = lane < head_dim

    def slot_loop(body):
        def step(s, _):
            body(s, pl.ds(pl.multiple_of(s * length, length), length))
            return 0

        lax.fori_loop(0, slots, step, 0)

    def part(s, k):
        return mod[pl.ds(s, 1), k * width : (k + 1) * width]

    def only(pair_block, first):
        return jnp.where(lower if first else jnp.logical_not(lower), pair_block, jnp.zeros_like(pair_block))

    def column_sum(values):
        return jnp.sum(values, axis=0, keepdims=True)

    def load_matrix(flat_ref, top, matrix):
        height, across = matrix.shape[0], matrix.shape[1] // LANES
        total = height * across

        def widen(t, _):
            at = pl.multiple_of(t * LANES, LANES)
            line[pl.ds(at, LANES), :] = flat_ref[pl.ds(top + at, LANES), :].astype(f32)
            return 0

        lax.fori_loop(0, total // LANES, widen, 0)
        for j in range(across):
            matrix[:, j * LANES : (j + 1) * LANES] = line[pl.ds(j, height, stride=across), :].astype(b16)

    def store_matrix(matrix, flat_ref, top):
        height, across = matrix.shape[0], matrix.shape[1] // LANES
        total = height * across
        for j in range(across):
            line[pl.ds(j, height, stride=across), :] = matrix[:, j * LANES : (j + 1) * LANES].astype(f32)

        def narrow(t, _):
            at = pl.multiple_of(t * LANES, LANES)
            flat_ref[pl.ds(top + at, LANES), :] = line[pl.ds(at, LANES), :].astype(b16)
            return 0

        lax.fori_loop(0, total // LANES, narrow, 0)

    proj_top, two_top = 3 * width * width // LANES, width * hidden // LANES
    load_matrix(attn_ref, 0, w_qkv)
    load_matrix(attn_ref, proj_top, w_proj)
    load_matrix(mlp_ref, 0, w_one)
    load_matrix(mlp_ref, two_top, w_two)
    cond = cond_ref[...]
    cond_act = (cond * jax.nn.sigmoid(cond)).astype(b16)
    mod[...] = dot(cond_act, w_ada[...]) + bias_ref[:, : 6 * width]

    def norm_first(s, rows):
        normed, inverse = layer_norm(x_ref[s])
        norm_one[rows, :] = normed
        inv_one[rows, :] = inverse
        h_one[rows, :] = (normed * (1.0 + part(s, 1)) + part(s, 0)).astype(b16)

    slot_loop(norm_first)
    for k, offset in enumerate((o_query, None, o_value)):
        cols = slice(k * width, (k + 1) * width)
        value = dot(h_one[...], w_qkv[:, cols])
        if offset is not None:
            value = value + bias_ref[:, offset : offset + width]
        qkv[:, cols] = value.astype(b16)

    def attend(s, rows):
        for pair in range(heads // 2):
            at = pair * 2 * head_dim
            query = qkv[rows, at : at + 2 * head_dim]
            key = qkv[rows, width + at : width + at + 2 * head_dim]
            value = qkv[rows, 2 * width + at : 2 * width + at + 2 * head_dim]
            halves = []
            for h in range(2):
                scores = dot(only(query, h == 0), key, (1, 1)) * score_scale
                total = jnp.log(jnp.sum(jnp.exp(scores), axis=-1, keepdims=True))
                prob = jnp.exp(scores - total)
                probs[s, 2 * pair + h] = prob
                halves.append(dot(prob.astype(b16), value))
            mixed[rows, at : at + 2 * head_dim] = jnp.where(lower, halves[0], halves[1]).astype(b16)

    slot_loop(attend)
    branch[...] = dot(mixed[...], w_proj[...]) + bias_ref[:, o_proj : o_proj + width]

    def norm_second(s, rows):
        after = x_ref[s] + part(s, 2) * branch[rows, :]
        dx[rows, :] = after
        normed, inverse = layer_norm(after)
        norm_two[rows, :] = normed
        inv_two[rows, :] = inverse
        h_two[rows, :] = (normed * (1.0 + part(s, 4)) + part(s, 3)).astype(b16)

    slot_loop(norm_second)

    def up(t, _):
        cols = pl.ds(pl.multiple_of(t * tile, tile), tile)
        shift = bias_ref[:, pl.ds(pl.multiple_of(o_one + t * tile, LANES), tile)]
        value = dot(h_two[...], w_one[:, cols]) + shift
        pre[:, cols] = value
        act[:, cols] = gelu_value(value).astype(b16)
        return 0

    lax.fori_loop(0, hidden // tile, up, 0)
    mlp[...] = dot(act[...], w_two[...]) + bias_ref[:, o_two : o_two + width]

    gbias_ref[...] = jnp.zeros_like(gbias_ref)

    def finish(s, rows):
        live = s < count
        value = mlp[rows, :]
        out_ref[s] = jnp.where(live, dx[rows, :] + part(s, 5) * value, 0.0)
        grad = jnp.where(live, cot_ref[s], 0.0)
        dmod[pl.ds(s, 1), 5 * width :] = column_sum(grad * value)
        full = grad * part(s, 5)
        gbias_ref[:, o_two : o_two + width] += column_sum(full)
        small[rows, :] = full.astype(b16)

    slot_loop(finish)

    def down(t, _):
        cols = pl.ds(pl.multiple_of(t * tile, tile), tile)
        full = dot(small[...], w_two[cols, :], (1, 1)) * gelu_slope(pre[:, cols])
        gbias_ref[:, pl.ds(pl.multiple_of(o_one + t * tile, LANES), tile)] = column_sum(full)
        grad = full.astype(b16)
        wide[:, cols] = grad
        g_two[cols, :] = dot(act[:, cols], small[...], (0, 0)).astype(g_two.dtype)
        g_one[:, cols] = dot(h_two[...], grad, (0, 0)).astype(g_one.dtype)
        return 0

    lax.fori_loop(0, hidden // tile, down, 0)
    back[...] = dot(wide[...], w_one[...], (1, 1))

    def mlp_back(s, rows):
        grad_two = back[rows, :]
        normed = norm_two[rows, :]
        dmod[pl.ds(s, 1), 4 * width : 5 * width] = column_sum(grad_two * normed)
        dmod[pl.ds(s, 1), 3 * width : 4 * width] = column_sum(grad_two)
        after = jnp.where(s < count, cot_ref[s], 0.0) + norm_backward(
            grad_two * (1.0 + part(s, 4)), normed, inv_two[rows, :]
        )
        dx[rows, :] = after
        dmod[pl.ds(s, 1), 2 * width : 3 * width] = column_sum(after * branch[rows, :])
        full = after * part(s, 2)
        gbias_ref[:, o_proj : o_proj + width] += column_sum(full)
        small[rows, :] = full.astype(b16)

    slot_loop(mlp_back)
    g_proj[...] = dot(mixed[...], small[...], (0, 0)).astype(g_proj.dtype)
    mixed[...] = dot(small[...], w_proj[...], (1, 1)).astype(b16)

    def attend_back(s, rows):
        for pair in range(heads // 2):
            at = pair * 2 * head_dim
            span = slice(at, at + 2 * head_dim)
            query = qkv[rows, span]
            key = qkv[rows, width + at : width + at + 2 * head_dim]
            value = qkv[rows, 2 * width + at : 2 * width + at + 2 * head_dim]
            grad = mixed[rows, span]
            d_query, d_key, d_value = [], [], []
            for h in range(2):
                prob = probs[s, 2 * pair + h]
                d_prob = dot(only(grad, h == 0), value, (1, 1))
                d_value.append(dot(prob.astype(b16), grad, (0, 0)))
                delta = jnp.sum(prob * d_prob, axis=-1, keepdims=True)
                d_score = (prob * (d_prob - delta) * score_scale).astype(b16)
                d_query.append(dot(d_score, key))
                d_key.append(dot(d_score, query, (0, 0)))
            d_query = jnp.where(lower, d_query[0], d_query[1]).astype(b16)
            d_key = jnp.where(lower, d_key[0], d_key[1]).astype(b16)
            d_value = jnp.where(lower, d_value[0], d_value[1]).astype(b16)
            dqkv[rows, span] = d_query
            dqkv[rows, width + at : width + at + 2 * head_dim] = d_key
            dqkv[rows, 2 * width + at : 2 * width + at + 2 * head_dim] = d_value
            gbias_ref[:, o_query + at : o_query + at + 2 * head_dim] += column_sum(d_query.astype(f32))
            gbias_ref[:, o_value + at : o_value + at + 2 * head_dim] += column_sum(d_value.astype(f32))

    slot_loop(attend_back)
    for k in range(3):
        cols = slice(k * width, (k + 1) * width)
        g_qkv[:, cols] = dot(h_one[...], dqkv[:, cols], (0, 0)).astype(g_qkv.dtype)
    back[...] = dot(dqkv[...], w_qkv[...], (1, 1))

    def attn_back(s, rows):
        grad_one = back[rows, :]
        normed = norm_one[rows, :]
        dmod[pl.ds(s, 1), width : 2 * width] = column_sum(grad_one * normed)
        dmod[pl.ds(s, 1), :width] = column_sum(grad_one)
        gx_ref[s] = dx[rows, :] + norm_backward(
            grad_one * (1.0 + part(s, 1)), normed, inv_one[rows, :]
        )

    slot_loop(attn_back)
    gbias_ref[:, : 6 * width] = column_sum(dmod[...])
    grad_mod = dmod[...].astype(b16)
    store_matrix(g_qkv, g_attn, 0)
    store_matrix(g_proj, g_attn, proj_top)
    store_matrix(g_one, g_mlp, 0)
    store_matrix(g_two, g_mlp, two_top)
    act_ref[...] = cond_act
    dmod_ref[...] = grad_mod
    gcond_ref[...] = dot(grad_mod, w_ada[...], (1, 1)) * silu_slope(cond)


def run_block(counts, latents, conditioning, cotangent, weights, biases):
    slots, length, width = latents.shape
    w_ada, attn, mlp = weights
    hidden = mlp.size // (2 * width)
    rows = slots * length
    f32, b16 = jnp.float32, jnp.bfloat16
    outs = [
        (latents.shape, f32), (latents.shape, f32), (conditioning.shape, f32),
        (conditioning.shape, b16), ((slots, 6 * width), b16),
        (attn.shape, b16), (mlp.shape, b16), (biases.shape, f32),
    ]
    matrices = [(width, 3 * width), (width, width), (width, hidden), (hidden, width)]
    scratch = [((max(h * w for h, w in matrices) // LANES, LANES), f32)]
    scratch += [(shape, b16) for shape in matrices + matrices]
    scratch += [
        ((slots, 6 * width), f32), ((rows, width), f32), ((rows, 1), f32), ((rows, width), b16),
        ((rows, 3 * width), b16), ((slots, HEADS, length, length), f32), ((rows, width), b16),
        ((rows, width), f32), ((rows, width), f32), ((rows, 1), f32), ((rows, width), b16),
        ((rows, hidden), f32), ((rows, hidden), b16), ((rows, width), f32), ((rows, hidden), b16),
        ((rows, width), f32), ((rows, width), f32), ((rows, width), b16), ((rows, 3 * width), b16),
        ((slots, 6 * width), f32),
    ]
    vmem = pl.BlockSpec(memory_space=pltpu.VMEM)
    return pl.pallas_call(
        block_kernel,
        out_shape=[jax.ShapeDtypeStruct(shape, kind) for shape, kind in outs],
        in_specs=[pl.BlockSpec(memory_space=pltpu.SMEM)] + [vmem] * 7,
        out_specs=[vmem] * len(outs),
        scratch_shapes=[pltpu.VMEM(shape, kind) for shape, kind in scratch],
        compiler_params=pltpu.CompilerParams(vmem_limit_bytes=60 * 1024 * 1024),
    )(counts, latents, conditioning, cotangent, *weights, biases)


def local(
    grid, latents, conditioning, counts, cotangent, ada_weights, attn_weights, mlp_weights, flat_biases
):
    model_width = latents.shape[-1]
    slots = latents.shape[0]
    shards = (ada_weights, attn_weights, mlp_weights, flat_biases)
    whole_ada, whole_attn, whole_mlp, whole_bias = gather_all(
        grid, [pack([shard], ()) for shard in shards]
    )
    bias_flat = whole_bias.reshape(grid.count, -1)[:, : flat_biases.shape[0]].reshape(-1)
    weights = (
        whole_ada.reshape(model_width, 6 * model_width),
        whole_attn.reshape(-1, LANES),
        whole_mlp.reshape(-1, LANES),
    )
    biases = bias_flat.astype(jnp.float32)[None]
    output, grad_latents, grad_conditioning, cond_act, grad_mod, g_attn, g_mlp, g_bias = (
        run_block(counts, latents, conditioning, cotangent, weights, biases)
    )

    gap = padded_rows(flat_biases.shape[0]) * LANES - flat_biases.shape[0]
    bias_lines = jnp.pad(
        g_bias.astype(jnp.bfloat16).reshape(grid.count, -1), ((0, 0), (0, gap))
    )
    all_mod, all_act, *sums = scatter_sum(
        grid,
        [flat.reshape(grid.sizes + (-1, LANES)) for flat in (g_attn, g_mlp, bias_lines)],
        [grad_mod, cond_act],
    )
    all_mod = all_mod.reshape(grid.count * slots, -1)
    all_act = all_act.reshape(grid.count * slots, -1)
    grads = [own_rows(all_act, all_mod, ada_weights.shape[0])]
    grads += [total.reshape(-1)[: shard.shape[0]] for total, shard in zip(sums, shards[1:])]
    return (output, grad_latents, grad_conditioning) + tuple(grads)


def own_rows(left, right, extent):
    wide = right.shape[1]
    start = lax.axis_index(AXES) * extent
    rows = min(-(-extent // wide) + (1 if extent % wide else 0), left.shape[1])
    top = jnp.minimum(start // wide, left.shape[1] - rows)
    part = lax.dynamic_slice_in_dim(left, top, rows, 1)
    whole = dot(part, right, (0, 0)).reshape(-1)
    if rows * wide == extent:
        return whole
    return lax.dynamic_slice_in_dim(whole, start - top * wide, extent, 0)


def solution(mesh):
    in_specs = (
        P(("dp", "fsdp"), None, None),
        P(("dp", "fsdp"), None),
        P(("dp", "fsdp")),
        P(("dp", "fsdp"), None, None),
        P(("dp", "fsdp")),
        P(("dp", "fsdp")),
        P(("dp", "fsdp")),
        P(("dp", "fsdp")),
    )
    out_specs = (
        P(("dp", "fsdp"), None, None),
        P(("dp", "fsdp"), None, None),
        P(("dp", "fsdp"), None),
        P(("dp", "fsdp")),
        P(("dp", "fsdp")),
        P(("dp", "fsdp")),
        P(("dp", "fsdp")),
    )
    return jax.shard_map(partial(local, Grid(mesh)), mesh=mesh, in_specs=in_specs, out_specs=out_specs, check_vma=False)
```
